128 devices in a mesh: dom: 4 (over x), brick: 32 (over z, y, core).
Axes of the slice: x: 4, y: 4, z: 4, core: 2. Of those that a mesh axis runs over, the one named last changes fastest.
Arguments:
- positions: float32 [3, 8192, 128], P(None, ('dom', 'brick')), may hold values from 0 to 1
- direction: float32 [3, 8192, 128], P(None, ('dom', 'brick')), may hold values from -6 to 6
- pair_local: int32 [32768], P(('dom', 'brick')), may hold values from 0 to 63
- pair_peer: int32 [32768, 1], P(('dom', 'brick')), may hold values from 0 to 127; in each aligned block of 256 rows (0 to 255, 256 to 511, ...) at most 4 rows name the same one
- pair_remote: int32 [32768], P(('dom', 'brick')), may hold values from 0 to 63
- pair_mask: int32 [32768, 128], P(('dom', 'brick')), may hold values 0 or 1
Outputs:
- gradient: float32 [3, 8192, 128], P(None, ('dom', 'brick'))
- hess_dir: float32 [3, 8192, 128], P(None, ('dom', 'brick'))
The draws below stay inside these ranges and needn't reach their ends.
Inputs may be any that keep to these rules, and one draw needn't show every extreme that they name: `pair_peer`: among the 256 rows of one device no device is named more than 4 times.
All inputs are finite; a program needn't handle non-finite values. No bound on the sum of `pair_mask` on one device may be relied on, other than what follows from the above.
Results may differ from the reference program's by a relative error of at most 0.0003.
Values sent between devices are 32-bit elements; how exact they have to be, the bound alone decides.
A program may use at most 64 MiB of HBM per device.

```python
import math
import jax
import jax.numpy as jnp
import numpy as np
from jax import lax

BS = 128
PAIRS_DEV = 256
BLK_DEV = 64
CAP = 4
BLOCKS = 8192
PAIRS = 32768
DEVICES = 128


def with_ends(drawn, rng, smallest, high):
    index_at = [jax.random.randint(jax.random.fold_in(rng, axis), (), 0, length) for axis, length in enumerate(drawn.shape)]
    main_axis = drawn.shape.index(max(drawn.shape))
    beside = index_at[:main_axis] + [(index_at[main_axis] + 1) % drawn.shape[main_axis]] + index_at[main_axis + 1:]
    return drawn.at[tuple(index_at)].set(smallest).at[tuple(beside)].set(high)


def level_of(rng, shape, shards, smallest, top_value):
    def one(axis_at, blocks):
        heights = jax.random.uniform(jax.random.fold_in(jax.random.fold_in(rng, 6), axis_at), (blocks,), jnp.float32, smallest / len(shards), top_value / len(shards))
        return jnp.repeat(jnp.exp(heights), shape[axis_at] // blocks).reshape((-1,) + (1,) * (len(shape) - axis_at - 1))

    level = one(*shards[0])
    for cut in shards[1:]:
        level = level * one(*cut)
    return level


def routed_block(key, own, number, rows, count, top, limit, slope):
    order = jax.random.permutation(key, count)
    crowded, usual = portions_of(count, rows * top, limit, slope, True), portions_of(count, rows * top, limit, slope, False)
    places = jnp.arange(count)

    def named(sizes, rotation):
        used = int((sizes > 0).sum())
        fixed = max(1, used // 4)
        moved = fixed + (places - fixed + rotation * (used - fixed)) % max(1, count - fixed)
        return jnp.zeros((count,), jnp.int32).at[order[jnp.where(places < fixed, places, moved)]].set(jnp.asarray(sizes, jnp.int32))

    sizes = jnp.where(number % 4 == 0, named(crowded, number // 4), named(usual, number - number // 4 - 1))
    mixed = jax.random.permutation(jax.random.fold_in(own, 3), count)
    giver, taker = mixed[0:count // 2 * 2:2], mixed[1:count // 2 * 2:2]
    margin = jnp.minimum(sizes[giver] - 1, limit - sizes[taker]) // 2
    margin = jnp.where((giver == order[0]) | (taker == order[0]) | (sizes[taker] == 0), 0, jnp.maximum(margin, 0))
    moved = jax.random.randint(jax.random.fold_in(own, 4), (count // 2,), 0, 1 << 20) % (margin + 1)
    sizes = sizes.at[giver].add(-moved).at[taker].add(moved)
    members = jnp.searchsorted(jnp.cumsum(sizes), jnp.arange(rows * top), side="right").astype(jnp.int32)
    table = members.reshape(top, rows).T
    table = table[jax.random.permutation(jax.random.fold_in(own, 1), rows)]
    rotation = jax.random.randint(jax.random.fold_in(own, 2), (rows, 1), 0, top)
    return jnp.take_along_axis(table, (jnp.arange(top)[None, :] + rotation) % top, axis=1)


def portions_of(amount, total, reach, lean, full):
    portions = [(1 << 20) // math.isqrt(grade ** lean) + 1 for grade in range(1, amount + 1)]
    largest = reach if full else min(reach, max(-(-total // amount), total * portions[0] // sum(portions)))
    least = 1 if total - largest >= amount - 1 else 0
    counts, spare = [largest] + [least] * (amount - 1), total - largest - least * (amount - 1)
    while spare > 0:
        movable = [i for i in range(1, amount) if counts[i] < largest] or [i for i in range(1, amount) if counts[i] < reach]
        whole, budget = sum([portions[i] for i in movable]), spare
        for i in movable:
            addition = min(reach - counts[i], max(1, budget * portions[i] // whole), spare)
            counts[i] = counts[i] + addition
            spare = spare - addition
    return np.array(counts)


def normal_values(key, shape, scale, most, pieces=(), dtype=jnp.bfloat16):
    drawn = jax.random.normal(key, shape, jnp.float32) * scale
    if len(pieces) > 0:
        drawn = level_of(key, shape, pieces, -0.22, 0.18) * drawn
    return jnp.clip(drawn, min=-most, max=most).astype(dtype)


def setup_inputs(seed: int = 0) -> dict:
    seeds = jax.random.split(jax.random.key(seed), 7)
    positions = jnp.clip(1.0 * jax.random.uniform(seeds[0], (3, BLOCKS, BS), jnp.float32) ** level_of(seeds[0], (3, BLOCKS, BS), ((1, 128),), -0.2, 0.2), 0.0, 1.0)
    direction = normal_values(seeds[1], (3, BLOCKS, BS), 1.0, 6.0, ((1, 128),), jnp.float32)
    pair_local = with_ends(jax.random.randint(seeds[2], (PAIRS,), 0, BLK_DEV), jax.random.fold_in(seeds[2], 1), 0, BLK_DEV - 1).astype(jnp.int32)
    pair_peer_keys = jax.random.split(jax.random.fold_in(seeds[3], 1), PAIRS // PAIRS_DEV)
    pair_peer_turns = jax.random.permutation(jax.random.fold_in(seeds[3], 3), PAIRS // PAIRS_DEV)
    pair_peer = jax.vmap(lambda own, number: routed_block(jax.random.fold_in(seeds[3], 2), own, number, PAIRS_DEV, DEVICES, 1, CAP, 2))(pair_peer_keys, pair_peer_turns).reshape((PAIRS, 1))
    pair_remote = with_ends(jax.random.randint(seeds[4], (PAIRS,), 0, BLK_DEV), jax.random.fold_in(seeds[4], 1), 0, BLK_DEV - 1).astype(jnp.int32)
    pair_mask = with_ends((jax.random.randint(seeds[5], (PAIRS, BS), 0, 4) < 3).astype(jnp.int32), jax.random.fold_in(seeds[5], 1), 0, 1)
    return {"positions": positions, "direction": direction, "pair_local": pair_local, "pair_peer": pair_peer, "pair_remote": pair_remote, "pair_mask": pair_mask}


thick = 0.1
kappa = 0.005


def tile_terms(own, partner, mask):
    r = own[:3, :, :, None] - partner[:3, :, None, :]
    s = jnp.sum(r * r, axis=0) + thick
    gap = s - 1.0
    logs = jnp.log(s)
    first = -2.0 * gap * logs - gap * gap / s
    second = -2.0 * logs - 4.0 * gap / s + gap * gap / (s * s)
    live = (s < 1.0) & (mask[:, :, None] > 0)
    w = own[3:, :, :, None] - partner[3:, :, None, :]
    c_one = jnp.where(live, 2.0 * kappa * first, 0.0)
    c_two = jnp.where(live, 4.0 * kappa * second * jnp.sum(r * w, axis=0), 0.0)
    grad_part = c_one * r
    hv_part = c_two * r + c_one * w
    both = jnp.concatenate([grad_part, hv_part], axis=0)
    return jnp.sum(both, axis=3), -jnp.sum(both, axis=2)


def reference(positions, direction, pair_local, pair_peer, pair_remote, pair_mask):
    total = pair_local.shape[0]
    owner = (jnp.arange(total) // PAIRS_DEV).astype(jnp.int32)
    left_block = (owner * BLK_DEV + pair_local).astype(jnp.int32)
    block_b = (pair_peer[:, 0] * BLK_DEV + pair_remote).astype(jnp.int32)
    data = jnp.concatenate([positions, direction], axis=0)
    batch = 64
    steps = total // batch
    index_a = left_block.reshape(steps, batch)
    index_b = block_b.reshape(steps, batch)
    masks = pair_mask.reshape(steps, batch, BS)

    def advance(acc, items):
        ia, ib, mk = items
        own = jnp.take(data, ia, axis=1)
        partner = jnp.take(data, ib, axis=1)
        left_term, right_term = tile_terms(own, partner, mk)
        acc = acc.at[:, ia].add(left_term)
        acc = acc.at[:, ib].add(right_term)
        return acc, None

    start = jnp.zeros(data.shape, jnp.float32)
    acc, _ = lax.scan(advance, start, (index_a, index_b, masks))
    return acc[:3], acc[3:]
```

```python
import functools
import math

import jax
import jax.numpy as jnp
from jax import lax
from jax.experimental import pallas as pl
from jax.experimental.pallas import tpu as pltpu
from jax.sharding import PartitionSpec as P

MESH = pl.DeviceIdType.MESH
AXES = ("dom", "brick")

F32, BF16 = jnp.float32, jnp.bfloat16
K1, K2C = -0.01, 0.02
KK = 80

def rows(values):
    it = lax.broadcasted_iota(jnp.int32, (8, 128), 0)
    out = jnp.zeros((8, 128), F32)
    for k, v in enumerate(values):
        if v != 0.0:
            out = jnp.where(it == k, F32(v), out)
    return out

def split3(z):
    h = z.astype(BF16).astype(F32)
    r = z - h
    m = r.astype(BF16).astype(F32)
    return h, m, r - m

def split2(z):
    h = z.astype(BF16)
    return h, (z - h.astype(F32)).astype(BF16)

NT = (((1,), (1,)), ((), ()))

def prepare(pos, dirn, own, f8, lhs, unroll=4):
    nb = pos.shape[1]
    x = [pos[c] - 0.5 for c in range(3)]
    u = [dirn[c] for c in range(3)]
    a = x[0]*x[0] + x[1]*x[1] + x[2]*x[2] + 0.1
    b = x[0]*u[0] + x[1]*u[1] + x[2]*u[2]
    one = jnp.ones_like(a)
    for k, v in enumerate(x + u + [one, jnp.zeros_like(a)]):
        own[:, k, :] = v
    for k, v in enumerate(x + [a, b] + u):
        f8[:, k, :] = v
    eye = (lax.broadcasted_iota(jnp.int32, (128, 128), 0) == lax.broadcasted_iota(jnp.int32, (128, 128), 1)).astype(BF16)
    ones3 = rows([1, 1, 1])
    zero = jnp.zeros((8, 128), F32)

    @pl.loop(0, nb // unroll)
    def _(g):
        for j in range(unroll):
            k = g * unroll + j
            h, m, l = split3(f8[k])
            fk = jnp.concatenate([h, h, m, m, h, l, ones3, ones3, ones3, zero], axis=0).astype(BF16)
            lhs[k] = lax.dot_general(eye, fk, NT, preferred_element_type=F32).astype(BF16)

def pairs_kernel(loc, slot, pos, dirn, mask, recv, acc, ret, own, f8, lhs, *, unroll, npairs):
    prepare(pos, dirn, own, f8, lhs)
    acc[...] = jnp.zeros_like(acc)
    it = lax.broadcasted_iota(jnp.int32, (8, 128), 0)
    center = rows([0.5, 0.5, 0.5])
    top = rows([0, 0, 0, 0, 0, 0, 1, 0])
    cp = rows([-2, -2, -2])
    e3 = rows([0, 0, 0, 1])
    e34 = rows([0, 0, 0, 1, 1])
    m35 = rows([0, 0, 0, K2C, K2C, K2C])
    zero = jnp.zeros((8, 128), F32)

    def side(z):
        h, m, l = split3(z)
        return [h, m, h, m, l, h]

    @pl.loop(0, npairs // unroll)
    def _(g):
        for j in range(unroll):
            p = g * unroll + j
            ia = loc[p]
            sl = slot[p]
            b = jnp.where(it < 6, recv[sl] - center, top)
            o = own[ia]
            mk = jnp.broadcast_to(mask[pl.ds(p, 1), :].astype(F32), (8, 128))
            ro = pltpu.roll(b, 5, 0)
            tp = list(split3(b * b))
            tq = list(split3(b * ro))
            rp = jnp.concatenate(side(b * cp + e3) + tp + [zero], axis=0).astype(BF16)
            rq = jnp.concatenate(side(e34 - ro) + tq + [zero], axis=0).astype(BF16)
            rhs = jnp.concatenate([rp, rq], axis=1)
            sq = jnp.dot(lhs[ia], rhs, preferred_element_type=F32)
            s = jnp.minimum(sq[:, :128], 1.0)
            q = sq[:, 128:]
            l2 = 2.0 * jnp.log(s)
            t = 1.0 - 1.0 / s
            c1 = (s - 1.0) * (l2 + t)
            c2 = (t * (t - 4.0) - l2) * q
            c1h, c1l = split2(c1)
            c2h, c2l = split2(c2)
            xh, xl = split3(o * mk)[:2]
            x16 = jnp.concatenate([xh, xl], axis=0).astype(BF16)
            yh, yl = split3(b)[:2]
            y16 = jnp.concatenate([yh, yl], axis=0).astype(BF16)
            cm = jnp.concatenate([jnp.concatenate([c1h, c2h], axis=1), jnp.concatenate([c1l, c2l], axis=1)], axis=0)
            rr = jnp.dot(jnp.concatenate([x16, x16], axis=1), cm, preferred_element_type=F32)
            rr = rr[:8] + rr[8:]
            cn = jnp.concatenate([jnp.concatenate([c1h, c1l], axis=1), jnp.concatenate([c2h, c2l], axis=1)], axis=0)
            ll = lax.dot_general(jnp.concatenate([y16, y16], axis=1), cn, NT, preferred_element_type=F32)
            ll = ll[:8] + ll[8:]
            r1, r2 = rr[:, :128], rr[:, 128:]
            d1 = r1 - b * jnp.broadcast_to(r1[6:7], (8, 128))
            d2 = r2 - b * jnp.broadcast_to(r2[6:7], (8, 128))
            ret[sl] = (-K1) * d1 - m35 * pltpu.roll(d2, 3, 0)
            l1, l2_ = ll[:, :128], ll[:, 128:]
            d1 = o * jnp.broadcast_to(l1[6:7], (8, 128)) - l1
            d2 = o * jnp.broadcast_to(l2_[6:7], (8, 128)) - l2_
            acc[ia] += mk * (K1 * d1 + m35 * pltpu.roll(d2, 3, 0))

UNROLL = 16


class Ring:
    def __init__(self, doms, bricks):
        side = math.isqrt(bricks // 2)
        self.doms, self.bricks, self.side = doms, bricks, side
        self.count = doms * bricks
        self.dom, self.brick = lax.axis_index("dom"), lax.axis_index("brick")
        self.me = self.dom * bricks + self.brick

    def at(self, step):
        x = step % self.doms
        rest = step // self.doms
        c = rest % 2
        y = (rest // 2) % self.side
        z = rest // (2 * self.side)
        dom = (self.dom + x) % self.doms
        low = self.brick % 2
        mid = (self.brick // 2) % self.side
        high = self.brick // (2 * self.side)
        brick = (
            ((high + z) % self.side) * (2 * self.side) + ((mid + y) % self.side) * 2 + (low + c) % 2
        )
        return (dom, brick), dom * self.bricks + brick


def enter(ring):
    barrier = pltpu.get_barrier_semaphore()

    @pl.loop(1, ring.count)
    def _(k):
        pl.semaphore_signal(barrier, inc=1, device_id=ring.at(k)[0], device_id_type=MESH)

    return barrier


def fetch_kernel(peer, remote, pos, dirn, recv, slot, asked_out, own, request, asked, table, scalars, send, sems, *, shape):
    ring = Ring(*shape)
    count, me = ring.count, ring.me
    cap = send.shape[1]
    npairs = peer.shape[0]
    barrier = enter(ring)

    for c in range(3):
        own[:, c, :] = pos[c]
        own[:, 3 + c, :] = dirn[c]
    lane = lax.broadcasted_iota(jnp.int32, (npairs, count), 1)
    hot = (peer[...] == lane).astype(F32).astype(BF16)
    eye = (
        lax.broadcasted_iota(jnp.int32, (count, count), 0)
        == lax.broadcasted_iota(jnp.int32, (count, count), 1)
    ).astype(F32).astype(BF16)
    turned = lax.dot_general(eye, hot, NT, preferred_element_type=F32)
    earlier = (
        lax.broadcasted_iota(jnp.int32, (npairs, npairs), 0)
        < lax.broadcasted_iota(jnp.int32, (npairs, npairs), 1)
    ).astype(F32).astype(BF16)
    before = jnp.dot(turned.astype(BF16), earlier, preferred_element_type=F32)
    device = lax.broadcasted_iota(jnp.int32, (count, npairs), 0).astype(F32)
    slot[...] = jnp.sum(turned * (device * cap + before), axis=0, keepdims=True).astype(jnp.int32)
    wanted = turned * (remote[...] + 1).astype(F32)
    column = lax.broadcasted_iota(jnp.int32, (count, 128), 1)
    out = jnp.zeros((count, 128), F32)
    for r in range(cap):
        named = jnp.sum(jnp.where(before == r, wanted, 0.0), axis=1, keepdims=True)
        out = jnp.where(column == r, named, out)
    request[...] = out
    pl.semaphore_wait(barrier, count - 1)

    @pl.loop(1, count)
    def _(k):
        to, index = ring.at(k)
        pltpu.make_async_remote_copy(
            src_ref=request.at[pl.ds(index, 1)], dst_ref=asked.at[pl.ds(me, 1)],
            send_sem=sems.at[0], recv_sem=sems.at[1], device_id=to, device_id_type=MESH,
        ).start()

    own_request = pltpu.make_async_copy(request.at[pl.ds(me, 1)], asked.at[pl.ds(me, 1)], sems.at[2])
    own_request.start()
    own_request.wait()
    rest = pltpu.make_async_remote_copy(
        src_ref=request.at[pl.ds(0, count - 1)], dst_ref=asked.at[pl.ds(0, count - 1)],
        send_sem=sems.at[0], recv_sem=sems.at[1], device_id=ring.at(1)[0], device_id_type=MESH,
    )
    rest.wait_recv()
    table[...] = asked[...].T[:8].astype(jnp.int32)
    asked_out[...] = table[...]
    to_scalars = pltpu.make_async_copy(table, scalars, sems.at[2])
    to_scalars.start()
    to_scalars.wait()

    def gather(index):
        for r in range(cap):
            send[index, r] = own[jnp.clip(scalars[r, index] - 1, 0, own.shape[0] - 1)]

    @pl.loop(1, count)
    def _(k):
        to, index = ring.at(k)
        gather(index)
        pltpu.make_async_remote_copy(
            src_ref=send.at[index, :, pl.ds(0, 6)], dst_ref=recv.at[me, :, pl.ds(0, 6)],
            send_sem=sems.at[3], recv_sem=sems.at[4], device_id=to, device_id_type=MESH,
        ).start()

    gather(me)
    kept = pltpu.make_async_copy(send.at[me, :, pl.ds(0, 6)], recv.at[me, :, pl.ds(0, 6)], sems.at[2])
    kept.start()
    kept.wait()
    rest.wait_send()
    every = pltpu.make_async_remote_copy(
        src_ref=send.at[pl.ds(0, count - 1), :, pl.ds(0, 6)], dst_ref=recv.at[pl.ds(0, count - 1), :, pl.ds(0, 6)],
        send_sem=sems.at[3], recv_sem=sems.at[4], device_id=ring.at(1)[0], device_id_type=MESH,
    )
    every.wait_recv()
    every.wait_send()


def give_kernel(ret, came, sems, *, shape):
    ring = Ring(*shape)
    count, me = ring.count, ring.me
    barrier = enter(ring)
    pl.semaphore_wait(barrier, count - 1)

    @pl.loop(1, count)
    def _(k):
        to, index = ring.at(k)
        pltpu.make_async_remote_copy(
            src_ref=ret.at[index, :, pl.ds(0, 6)], dst_ref=came.at[me, :, pl.ds(0, 6)],
            send_sem=sems.at[0], recv_sem=sems.at[1], device_id=to, device_id_type=MESH,
        ).start()

    kept = pltpu.make_async_copy(ret.at[me, :, pl.ds(0, 6)], came.at[me, :, pl.ds(0, 6)], sems.at[2])
    kept.start()
    kept.wait()
    every = pltpu.make_async_remote_copy(
        src_ref=ret.at[pl.ds(0, count - 1), :, pl.ds(0, 6)], dst_ref=came.at[pl.ds(0, count - 1), :, pl.ds(0, 6)],
        send_sem=sems.at[0], recv_sem=sems.at[1], device_id=ring.at(1)[0], device_id_type=MESH,
    )
    every.wait_recv()
    every.wait_send()


def add_kernel(asked, acc, came, grad, hess, parts, *, cap):
    blocks = acc.shape[0]
    parts[...] = jnp.zeros_like(parts)

    @pl.loop(0, came.shape[0], unroll=4)
    def _(d):
        for r in range(cap):
            a = asked[r, d]
            k = jnp.where(a > 0, a - 1, blocks)
            parts[r, k] += came[d, r]

    total = acc[...]
    for r in range(cap):
        total = total + parts[r, :blocks]
    parts[0, :blocks] = total
    for c in range(3):
        grad[c] = parts[0, :blocks, c]
        hess[c] = parts[0, :blocks, 3 + c]


def on_device(positions, direction, pair_local, pair_peer, pair_remote, pair_mask, *, shape):
    npairs = pair_local.shape[0]
    nblocks, width = positions.shape[1:]
    count = shape[0] * shape[1]
    cap = max(2, 2 * npairs // count)
    V = pl.BlockSpec(memory_space=pltpu.VMEM)
    S = pl.BlockSpec(memory_space=pltpu.SMEM)
    A = pl.BlockSpec(memory_space=pl.ANY)
    DMA = pltpu.SemaphoreType.DMA
    pairs_shape = jax.ShapeDtypeStruct((count, cap, 8, width), F32)
    params = functools.partial(pltpu.CompilerParams, vmem_limit_bytes=56 * 2**20)
    recv, slot, asked = pl.pallas_call(
        functools.partial(fetch_kernel, shape=shape),
        out_shape=(
            pairs_shape,
            jax.ShapeDtypeStruct((1, npairs), jnp.int32),
            jax.ShapeDtypeStruct((8, count), jnp.int32),
        ),
        in_specs=[V, V, V, V],
        out_specs=(A, V, V),
        scratch_shapes=[
            pltpu.VMEM((nblocks, 8, width), F32),
            pltpu.VMEM((count, 128), F32),
            pltpu.VMEM((count, 128), F32),
            pltpu.VMEM((8, count), jnp.int32),
            pltpu.SMEM((8, count), jnp.int32),
            pltpu.VMEM((count, cap, 8, width), F32),
            DMA((5,)),
        ],
        compiler_params=params(collective_id=0, has_side_effects=True),
        name="fetch",
    )(pair_peer, pair_remote.reshape(1, npairs), positions, direction)
    acc, ret = pl.pallas_call(
        functools.partial(pairs_kernel, unroll=UNROLL, npairs=npairs),
        out_shape=(
            jax.ShapeDtypeStruct((nblocks, 8, width), F32),
            jax.ShapeDtypeStruct((count * cap, 8, width), F32),
        ),
        in_specs=[S, S, V, V, V, V],
        out_specs=(V, V),
        scratch_shapes=[
            pltpu.VMEM((nblocks, 8, width), F32),
            pltpu.VMEM((nblocks, 8, width), F32),
            pltpu.VMEM((nblocks, width, KK), BF16),
        ],
        compiler_params=params(),
        name="pairs",
    )(
        pair_local, slot.reshape(npairs), positions, direction, pair_mask,
        recv.reshape(count * cap, 8, width),
    )
    came = pl.pallas_call(
        functools.partial(give_kernel, shape=shape),
        out_shape=pairs_shape,
        in_specs=[A],
        out_specs=A,
        scratch_shapes=[DMA((3,))],
        compiler_params=params(collective_id=1, has_side_effects=True),
        name="give",
    )(ret.reshape(count, cap, 8, width))
    half = jax.ShapeDtypeStruct((3, nblocks, width), F32)
    return pl.pallas_call(
        functools.partial(add_kernel, cap=cap),
        out_shape=(half, half),
        in_specs=[S, V, V],
        out_specs=(V, V),
        scratch_shapes=[pltpu.VMEM((cap, nblocks + 1, 8, width), F32)],
        compiler_params=params(),
        name="add",
    )(asked, acc, came)


def solution(mesh):
    shape = (mesh.shape["dom"], mesh.shape["brick"])
    rows_of = P(None, AXES, None)
    return jax.shard_map(
        functools.partial(on_device, shape=shape),
        mesh=mesh,
        in_specs=(rows_of, rows_of, P(AXES), P(AXES, None), P(AXES), P(AXES, None)),
        out_specs=(rows_of, rows_of),
        check_vma=False,
    )
```

```python
import functools
import math
import random

import jax
import jax.numpy as jnp
from jax import lax
from jax.experimental import pallas as pl
from jax.experimental.pallas import tpu as pltpu
from jax.sharding import PartitionSpec as P

MESH = pl.DeviceIdType.MESH
AXES = ("dom", "brick")

F32, BF16 = jnp.float32, jnp.bfloat16
K1, K2C = -0.01, 0.02
KK = 80

def rows(values):
    it = lax.broadcasted_iota(jnp.int32, (8, 128), 0)
    out = jnp.zeros((8, 128), F32)
    for k, v in enumerate(values):
        if v != 0.0:
            out = jnp.where(it == k, F32(v), out)
    return out

def split3(z):
    h = z.astype(BF16).astype(F32)
    r = z - h
    m = r.astype(BF16).astype(F32)
    return h, m, r - m

def split2(z):
    h = z.astype(BF16)
    return h, (z - h.astype(F32)).astype(BF16)

NT = (((1,), (1,)), ((), ()))

def prepare(pos, dirn, own, f8, lhs, unroll=4):
    nb = pos.shape[1]
    x = [pos[c] - 0.5 for c in range(3)]
    u = [dirn[c] for c in range(3)]
    a = x[0]*x[0] + x[1]*x[1] + x[2]*x[2] + 0.1
    b = x[0]*u[0] + x[1]*u[1] + x[2]*u[2]
    one = jnp.ones_like(a)
    for k, v in enumerate(x + u + [one, jnp.zeros_like(a)]):
        own[:, k, :] = v
    for k, v in enumerate(x + [a, b] + u):
        f8[:, k, :] = v
    eye = (lax.broadcasted_iota(jnp.int32, (128, 128), 0) == lax.broadcasted_iota(jnp.int32, (128, 128), 1)).astype(BF16)
    ones3 = rows([1, 1, 1])
    zero = jnp.zeros((8, 128), F32)

    @pl.loop(0, nb // unroll)
    def _(g):
        for j in range(unroll):
            k = g * unroll + j
            h, m, l = split3(f8[k])
            fk = jnp.concatenate([h, h, m, m, h, l, ones3, ones3, ones3, zero], axis=0).astype(BF16)
            lhs[k] = lax.dot_general(eye, fk, NT, preferred_element_type=F32).astype(BF16)

def pairs_kernel(loc, slot, pos, dirn, mask, recv, acc, ret, own, f8, lhs, *, unroll, npairs):
    prepare(pos, dirn, own, f8, lhs)
    acc[...] = jnp.zeros_like(acc)
    it = lax.broadcasted_iota(jnp.int32, (8, 128), 0)
    center = rows([0.5, 0.5, 0.5])
    top = rows([0, 0, 0, 0, 0, 0, 1, 0])
    cp = rows([-2, -2, -2])
    e3 = rows([0, 0, 0, 1])
    e34 = rows([0, 0, 0, 1, 1])
    m35 = rows([0, 0, 0, K2C, K2C, K2C])
    zero = jnp.zeros((8, 128), F32)

    def side(z):
        h, m, l = split3(z)
        return [h, m, h, m, l, h]

    @pl.loop(0, npairs // unroll)
    def _(g):
        for j in range(unroll):
            p = g * unroll + j
            ia = loc[p]
            sl = slot[p]
            b = jnp.where(it < 6, recv[sl] - center, top)
            o = own[ia]
            mk = jnp.broadcast_to(mask[pl.ds(p, 1), :].astype(F32), (8, 128))
            ro = pltpu.roll(b, 5, 0)
            tp = list(split3(b * b))
            tq = list(split3(b * ro))
            rp = jnp.concatenate(side(b * cp + e3) + tp + [zero], axis=0).astype(BF16)
            rq = jnp.concatenate(side(e34 - ro) + tq + [zero], axis=0).astype(BF16)
            rhs = jnp.concatenate([rp, rq], axis=1)
            sq = jnp.dot(lhs[ia], rhs, preferred_element_type=F32)
            s = jnp.minimum(sq[:, :128], 1.0)
            q = sq[:, 128:]
            l2 = 2.0 * jnp.log(s)
            t = 1.0 - 1.0 / s
            c1 = (s - 1.0) * (l2 + t)
            c2 = (t * (t - 4.0) - l2) * q
            c1h, c1l = split2(c1)
            c2h, c2l = split2(c2)
            xh, xl = split3(o * mk)[:2]
            x16 = jnp.concatenate([xh, xl], axis=0).astype(BF16)
            yh, yl = split3(b)[:2]
            y16 = jnp.concatenate([yh, yl], axis=0).astype(BF16)
            cm = jnp.concatenate([jnp.concatenate([c1h, c2h], axis=1), jnp.concatenate([c1l, c2l], axis=1)], axis=0)
            rr = jnp.dot(jnp.concatenate([x16, x16], axis=1), cm, preferred_element_type=F32)
            rr = rr[:8] + rr[8:]
            cn = jnp.concatenate([jnp.concatenate([c1h, c1l], axis=1), jnp.concatenate([c2h, c2l], axis=1)], axis=0)
            ll = lax.dot_general(jnp.concatenate([y16, y16], axis=1), cn, NT, preferred_element_type=F32)
            ll = ll[:8] + ll[8:]
            r1, r2 = rr[:, :128], rr[:, 128:]
            d1 = r1 - b * jnp.broadcast_to(r1[6:7], (8, 128))
            d2 = r2 - b * jnp.broadcast_to(r2[6:7], (8, 128))
            ret[sl] = (-K1) * d1 - m35 * pltpu.roll(d2, 3, 0)
            l1, l2_ = ll[:, :128], ll[:, 128:]
            d1 = o * jnp.broadcast_to(l1[6:7], (8, 128)) - l1
            d2 = o * jnp.broadcast_to(l2_[6:7], (8, 128)) - l2_
            acc[ia] += mk * (K1 * d1 + m35 * pltpu.roll(d2, 3, 0))

UNROLL = 16


class Ring:
    def __init__(self, doms, bricks):
        side = math.isqrt(bricks // 2)
        self.doms, self.bricks, self.side = doms, bricks, side
        self.count = doms * bricks
        self.dom, self.brick = lax.axis_index("dom"), lax.axis_index("brick")
        self.me = self.dom * bricks + self.brick
        self.core = self.brick % 2
        self.y = (self.brick // 2) % side
        self.z = self.brick // (2 * side)
        places = [(x, y, z) for x in range(doms) for y in range(side) for z in range(side)]
        hops = lambda place: sum(min(v, n - v) for v, n in zip(place, (doms, side, side)))
        random.Random(1).shuffle(places)
        places.sort(key=hops, reverse=True)
        self.others = [(*place, c) for place in places for c in range(2) if (*place, c) != (0, 0, 0, 0)]

    def at(self, place):
        x, y, z, c = place
        dom = (self.dom + x) % self.doms
        brick = (
            ((self.z + z) % self.side) * (2 * self.side) + ((self.y + y) % self.side) * 2 + (self.core + c) % 2
        )
        return (dom, brick), dom * self.bricks + brick


def enter(ring):
    barrier = pltpu.get_barrier_semaphore()

    for place in ring.others:
        pl.semaphore_signal(barrier, inc=1, device_id=ring.at(place)[0], device_id_type=MESH)

    return barrier


def fetch_kernel(peer, remote, pos, dirn, recv, slot, asked_out, own, request, asked, table, scalars, send, sems, *, shape):
    ring = Ring(*shape)
    count, me = ring.count, ring.me
    cap = send.shape[1]
    npairs = peer.shape[0]
    barrier = enter(ring)

    for c in range(3):
        own[:, c, :] = pos[c]
        own[:, 3 + c, :] = dirn[c]
    lane = lax.broadcasted_iota(jnp.int32, (npairs, count), 1)
    hot = (peer[...] == lane).astype(F32).astype(BF16)
    eye = (
        lax.broadcasted_iota(jnp.int32, (count, count), 0)
        == lax.broadcasted_iota(jnp.int32, (count, count), 1)
    ).astype(F32).astype(BF16)
    turned = lax.dot_general(eye, hot, NT, preferred_element_type=F32)
    earlier = (
        lax.broadcasted_iota(jnp.int32, (npairs, npairs), 0)
        < lax.broadcasted_iota(jnp.int32, (npairs, npairs), 1)
    ).astype(F32).astype(BF16)
    before = jnp.dot(turned.astype(BF16), earlier, preferred_element_type=F32)
    device = lax.broadcasted_iota(jnp.int32, (count, npairs), 0).astype(F32)
    slot[...] = jnp.sum(turned * (device * cap + before), axis=0, keepdims=True).astype(jnp.int32)
    wanted = turned * (remote[...] + 1).astype(F32)
    column = lax.broadcasted_iota(jnp.int32, (count, 128), 1)
    out = jnp.zeros((count, 128), F32)
    for r in range(cap):
        named = jnp.sum(jnp.where(before == r, wanted, 0.0), axis=1, keepdims=True)
        out = jnp.where(column == r, named, out)
    request[...] = out
    pl.semaphore_wait(barrier, count - 1)

    for place in ring.others:
        to, index = ring.at(place)
        pltpu.make_async_remote_copy(
            src_ref=request.at[pl.ds(index, 1)], dst_ref=asked.at[pl.ds(me, 1)],
            send_sem=sems.at[0], recv_sem=sems.at[1], device_id=to, device_id_type=MESH,
        ).start()

    own_request = pltpu.make_async_copy(request.at[pl.ds(me, 1)], asked.at[pl.ds(me, 1)], sems.at[2])
    own_request.start()
    own_request.wait()
    rest = pltpu.make_async_remote_copy(
        src_ref=request.at[pl.ds(0, count - 1)], dst_ref=asked.at[pl.ds(0, count - 1)],
        send_sem=sems.at[0], recv_sem=sems.at[1], device_id=ring.at(ring.others[0])[0], device_id_type=MESH,
    )
    rest.wait_recv()
    table[...] = asked[...].T[:8].astype(jnp.int32)
    asked_out[...] = table[...]
    to_scalars = pltpu.make_async_copy(table, scalars, sems.at[2])
    to_scalars.start()
    to_scalars.wait()

    def gather(index):
        for r in range(cap):
            send[index, r] = own[jnp.clip(scalars[r, index] - 1, 0, own.shape[0] - 1)]

    for place in ring.others:
        to, index = ring.at(place)
        gather(index)
        pltpu.make_async_remote_copy(
            src_ref=send.at[index, :, pl.ds(0, 6)], dst_ref=recv.at[me, :, pl.ds(0, 6)],
            send_sem=sems.at[3], recv_sem=sems.at[4], device_id=to, device_id_type=MESH,
        ).start()

    gather(me)
    kept = pltpu.make_async_copy(send.at[me, :, pl.ds(0, 6)], recv.at[me, :, pl.ds(0, 6)], sems.at[2])
    kept.start()
    kept.wait()
    rest.wait_send()
    every = pltpu.make_async_remote_copy(
        src_ref=send.at[pl.ds(0, count - 1), :, pl.ds(0, 6)], dst_ref=recv.at[pl.ds(0, count - 1), :, pl.ds(0, 6)],
        send_sem=sems.at[3], recv_sem=sems.at[4], device_id=ring.at(ring.others[0])[0], device_id_type=MESH,
    )
    every.wait_recv()
    every.wait_send()


def give_kernel(ret, came, sems, *, shape):
    ring = Ring(*shape)
    count, me = ring.count, ring.me
    barrier = enter(ring)
    pl.semaphore_wait(barrier, count - 1)

    for place in ring.others:
        to, index = ring.at(place)
        pltpu.make_async_remote_copy(
            src_ref=ret.at[index, :, pl.ds(0, 6)], dst_ref=came.at[me, :, pl.ds(0, 6)],
            send_sem=sems.at[0], recv_sem=sems.at[1], device_id=to, device_id_type=MESH,
        ).start()

    kept = pltpu.make_async_copy(ret.at[me, :, pl.ds(0, 6)], came.at[me, :, pl.ds(0, 6)], sems.at[2])
    kept.start()
    kept.wait()
    every = pltpu.make_async_remote_copy(
        src_ref=ret.at[pl.ds(0, count - 1), :, pl.ds(0, 6)], dst_ref=came.at[pl.ds(0, count - 1), :, pl.ds(0, 6)],
        send_sem=sems.at[0], recv_sem=sems.at[1], device_id=ring.at(ring.others[0])[0], device_id_type=MESH,
    )
    every.wait_recv()
    every.wait_send()


def add_kernel(asked, acc, came, grad, hess, parts, *, cap):
    blocks = acc.shape[0]
    parts[...] = jnp.zeros_like(parts)

    @pl.loop(0, came.shape[0], unroll=4)
    def _(d):
        for r in range(cap):
            a = asked[r, d]
            k = jnp.where(a > 0, a - 1, blocks)
            parts[r, k] += came[d, r]

    total = acc[...]
    for r in range(cap):
        total = total + parts[r, :blocks]
    parts[0, :blocks] = total
    for c in range(3):
        grad[c] = parts[0, :blocks, c]
        hess[c] = parts[0, :blocks, 3 + c]


def on_device(positions, direction, pair_local, pair_peer, pair_remote, pair_mask, *, shape):
    npairs = pair_local.shape[0]
    nblocks, width = positions.shape[1:]
    count = shape[0] * shape[1]
    cap = max(2, 2 * npairs // count)
    V = pl.BlockSpec(memory_space=pltpu.VMEM)
    S = pl.BlockSpec(memory_space=pltpu.SMEM)
    A = pl.BlockSpec(memory_space=pl.ANY)
    DMA = pltpu.SemaphoreType.DMA
    pairs_shape = jax.ShapeDtypeStruct((count, cap, 8, width), F32)
    params = functools.partial(pltpu.CompilerParams, vmem_limit_bytes=56 * 2**20)
    recv, slot, asked = pl.pallas_call(
        functools.partial(fetch_kernel, shape=shape),
        out_shape=(
            pairs_shape,
            jax.ShapeDtypeStruct((1, npairs), jnp.int32),
            jax.ShapeDtypeStruct((8, count), jnp.int32),
        ),
        in_specs=[V, V, V, V],
        out_specs=(A, V, V),
        scratch_shapes=[
            pltpu.VMEM((nblocks, 8, width), F32),
            pltpu.VMEM((count, 128), F32),
            pltpu.VMEM((count, 128), F32),
            pltpu.VMEM((8, count), jnp.int32),
            pltpu.SMEM((8, count), jnp.int32),
            pltpu.VMEM((count, cap, 8, width), F32),
            DMA((5,)),
        ],
        compiler_params=params(collective_id=0, has_side_effects=True),
        name="fetch",
    )(pair_peer, pair_remote.reshape(1, npairs), positions, direction)
    acc, ret = pl.pallas_call(
        functools.partial(pairs_kernel, unroll=UNROLL, npairs=npairs),
        out_shape=(
            jax.ShapeDtypeStruct((nblocks, 8, width), F32),
            jax.ShapeDtypeStruct((count * cap, 8, width), F32),
        ),
        in_specs=[S, S, V, V, V, V],
        out_specs=(V, V),
        scratch_shapes=[
            pltpu.VMEM((nblocks, 8, width), F32),
            pltpu.VMEM((nblocks, 8, width), F32),
            pltpu.VMEM((nblocks, width, KK), BF16),
        ],
        compiler_params=params(),
        name="pairs",
    )(
        pair_local, slot.reshape(npairs), positions, direction, pair_mask,
        recv.reshape(count * cap, 8, width),
    )
    came = pl.pallas_call(
        functools.partial(give_kernel, shape=shape),
        out_shape=pairs_shape,
        in_specs=[A],
        out_specs=A,
        scratch_shapes=[DMA((3,))],
        compiler_params=params(collective_id=1, has_side_effects=True),
        name="give",
    )(ret.reshape(count, cap, 8, width))
    half = jax.ShapeDtypeStruct((3, nblocks, width), F32)
    return pl.pallas_call(
        functools.partial(add_kernel, cap=cap),
        out_shape=(half, half),
        in_specs=[S, V, V],
        out_specs=(V, V),
        scratch_shapes=[pltpu.VMEM((cap, nblocks + 1, 8, width), F32)],
        compiler_params=params(),
        name="add",
    )(asked, acc, came)


def solution(mesh):
    shape = (mesh.shape["dom"], mesh.shape["brick"])
    rows_of = P(None, AXES, None)
    return jax.shard_map(
        functools.partial(on_device, shape=shape),
        mesh=mesh,
        in_specs=(rows_of, rows_of, P(AXES), P(AXES, None), P(AXES), P(AXES, None)),
        out_specs=(rows_of, rows_of),
        check_vma=False,
    )
```

```python
import functools
import math
import random

import jax
import jax.numpy as jnp
from jax import lax
from jax.experimental import pallas as pl
from jax.experimental.pallas import tpu as pltpu
from jax.sharding import PartitionSpec as P

MESH = pl.DeviceIdType.MESH
AXES = ("dom", "brick")

F32, BF16 = jnp.float32, jnp.bfloat16
K1, K2C = -0.01, 0.02
KK = 80

def rows(values):
    it = lax.broadcasted_iota(jnp.int32, (8, 128), 0)
    out = jnp.zeros((8, 128), F32)
    for k, v in enumerate(values):
        if v != 0.0:
            out = jnp.where(it == k, F32(v), out)
    return out

def split3(z):
    h = z.astype(BF16).astype(F32)
    r = z - h
    m = r.astype(BF16).astype(F32)
    return h, m, r - m

def split2(z):
    h = z.astype(BF16)
    return h, (z - h.astype(F32)).astype(BF16)

NT = (((1,), (1,)), ((), ()))

def prepare(pos, dirn, own, f8, lhs, unroll=4):
    nb = pos.shape[1]
    x = [pos[c] - 0.5 for c in range(3)]
    u = [dirn[c] for c in range(3)]
    a = x[0]*x[0] + x[1]*x[1] + x[2]*x[2] + 0.1
    b = x[0]*u[0] + x[1]*u[1] + x[2]*u[2]
    one = jnp.ones_like(a)
    for k, v in enumerate(x + u + [one, jnp.zeros_like(a)]):
        own[:, k, :] = v
    for k, v in enumerate(x + [a, b] + u):
        f8[:, k, :] = v
    eye = (lax.broadcasted_iota(jnp.int32, (128, 128), 0) == lax.broadcasted_iota(jnp.int32, (128, 128), 1)).astype(BF16)
    ones3 = rows([1, 1, 1])
    zero = jnp.zeros((8, 128), F32)

    @pl.loop(0, nb // unroll)
    def _(g):
        for j in range(unroll):
            k = g * unroll + j
            h, m, l = split3(f8[k])
            fk = jnp.concatenate([h, h, m, m, h, l, ones3, ones3, ones3, zero], axis=0).astype(BF16)
            lhs[k] = lax.dot_general(eye, fk, NT, preferred_element_type=F32).astype(BF16)

GROUP = 8


def pairs_kernel(loc, slot, pos, dirn, mask, recv, acc, ret, own, f8, lhs, *bufs, npairs):
    prepare(pos, dirn, own, f8, lhs)
    acc[...] = jnp.zeros_like(acc)
    sq, cs, ws = bufs[0:2], bufs[2:4], bufs[4:6]
    cs[1][...] = jnp.zeros_like(cs[1])
    ws[1][...] = jnp.zeros_like(ws[1])
    it = lax.broadcasted_iota(jnp.int32, (8, 128), 0)
    lane = lax.broadcasted_iota(jnp.int32, (128, 128), 1)
    center = rows([0.5, 0.5, 0.5])
    top = rows([0, 0, 0, 0, 0, 0, 1])
    cp = rows([-2, -2, -2])
    e3 = rows([0, 0, 0, 1])
    e34 = rows([0, 0, 0, 1, 1])
    last = rows([0, 0, 0, 0, 0, 0, 0, 1])
    m35 = rows([0, 0, 0, 1, 1, 1])
    zero = jnp.zeros((8, 128), F32)
    groups = npairs // GROUP

    def whole(row):
        return jnp.broadcast_to(row, (8, 128))

    def side(z):
        h, m, l = split3(z)
        return [h, m, h, m, l, h]

    def halves(z):
        h, l, _ = split3(z)
        return jnp.concatenate([h, l], axis=0).astype(BF16)

    def other(p):
        return jnp.where(it < 6, recv[slot[p]] - center, top)

    def active(p):
        return whole(mask[pl.ds(p, 1), :].astype(F32))

    def distances(g, out, js=range(GROUP)):
        for j in js:
            p = g * GROUP + j
            b = other(p)
            ro = pltpu.roll(b, 5, 0)
            rp = jnp.concatenate(side(b * cp + e3) + list(split3(b * b)) + [zero], axis=0).astype(BF16)
            rq = jnp.concatenate(side(e34 - ro) + list(split3(b * ro)) + [zero], axis=0).astype(BF16)
            out[pl.ds(128 * j, 128), :] = jnp.dot(
                lhs[loc[p]], jnp.concatenate([rp, rq], axis=1), preferred_element_type=F32
            )

    def factors(g, given, c, w, js=range(GROUP)):
        for j in js:
            p = g * GROUP + j
            b = other(p)
            rs = pl.ds(128 * j, 128)
            s = jnp.minimum(given[rs, 0:128], 1.0)
            l2 = 2.0 * jnp.log(s)
            t = 1.0 - 1.0 / s
            c1h, c1l = split2((s - 1.0) * (l2 + t))
            c2h, c2l = split2((t * (t - 4.0) - l2) * given[rs, 128:256])
            c[pl.ds(256 * j, 128), 0:128] = c1h
            c[pl.ds(256 * j, 128), 128:256] = c2h
            c[pl.ds(256 * j + 128, 128), 0:128] = c1l
            c[pl.ds(256 * j + 128, 128), 128:256] = c2l
            x = halves(own[loc[p]] * active(p))
            r = jnp.dot(jnp.concatenate([x, x], axis=1), c[pl.ds(256 * j, 256), :], preferred_element_type=F32)
            r = r[:8] + r[8:]
            r1, r2 = r[:, :128], r[:, 128:]
            d1 = r1 - b * whole(r1[6:7])
            d2 = r2 - b * whole(r2[6:7])
            ret[slot[p]] = (-K1) * d1 - K2C * m35 * pltpu.roll(d2, 3, 0)
            w[pl.ds(16 * j, 16), 0:128] = halves(K1 * b)
            w[pl.ds(16 * j, 16), 128:256] = halves(K2C * (m35 * pltpu.roll(b, 3, 0) + last))

    def residents(g, c, w):
        res = lax.dot_general(c[...], w[...], NT, preferred_element_type=F32)
        tot = res[:128] + res[128:256]
        for j in range(1, GROUP):
            tot = jnp.where(lane >= 16 * j, res[256 * j:256 * j + 128] + res[256 * j + 128:256 * j + 256], tot)
        tr = tot.T
        for j in range(GROUP):
            p = g * GROUP + j
            ia = loc[p]
            o = own[ia]
            sums = tr[16 * j:16 * j + 8] + tr[16 * j + 8:16 * j + 16]
            term = o * whole(sums[6:7]) + m35 * pltpu.roll(o, 3, 0) * whole(sums[7:8]) - sums
            acc[ia] += active(p) * term

    distances(0, sq[0])

    @pl.loop(0, groups // 8)
    def _(h):
        for k in range(8):
            odd = k % 2
            g = 8 * h + k
            residents(jnp.maximum(g - 1, 0), cs[1 - odd], ws[1 - odd])
            for j in range(GROUP):
                distances(jnp.minimum(g + 1, groups - 1), sq[1 - odd], [j])
                factors(g, sq[odd], cs[odd], ws[odd], [j])

    residents(groups - 1, cs[1], ws[1])


PAIR_BUFFERS = (
    [pltpu.VMEM((128 * GROUP, 256), F32)] * 2
    + [pltpu.VMEM((256 * GROUP, 256), BF16)] * 2
    + [pltpu.VMEM((16 * GROUP, 256), BF16)] * 2
)


class Ring:
    def __init__(self, doms, bricks):
        side = math.isqrt(bricks // 2)
        self.doms, self.bricks, self.side = doms, bricks, side
        self.count = doms * bricks
        self.dom, self.brick = lax.axis_index("dom"), lax.axis_index("brick")
        self.me = self.dom * bricks + self.brick
        self.core = self.brick % 2
        self.y = (self.brick // 2) % side
        self.z = self.brick // (2 * side)
        places = [(x, y, z) for x in range(doms) for y in range(side) for z in range(side)]
        hops = lambda place: sum(min(v, n - v) for v, n in zip(place, (doms, side, side)))
        random.Random(1).shuffle(places)
        places.sort(key=hops, reverse=True)
        self.others = [(*place, c) for place in places for c in range(2) if (*place, c) != (0, 0, 0, 0)]

    def at(self, place):
        x, y, z, c = place
        dom = (self.dom + x) % self.doms
        brick = (
            ((self.z + z) % self.side) * (2 * self.side) + ((self.y + y) % self.side) * 2 + (self.core + c) % 2
        )
        return (dom, brick), dom * self.bricks + brick


def enter(ring):
    barrier = pltpu.get_barrier_semaphore()

    for place in ring.others:
        pl.semaphore_signal(barrier, inc=1, device_id=ring.at(place)[0], device_id_type=MESH)

    return barrier


def fetch_kernel(peer, remote, pos, dirn, recv, slot, asked_out, own, request, asked, table, scalars, send, sems, *, shape):
    ring = Ring(*shape)
    count, me = ring.count, ring.me
    cap = send.shape[1]
    npairs = peer.shape[0]
    barrier = enter(ring)

    for c in range(3):
        own[:, c, :] = pos[c]
        own[:, 3 + c, :] = dirn[c]
    lane = lax.broadcasted_iota(jnp.int32, (npairs, count), 1)
    hot = (peer[...] == lane).astype(F32).astype(BF16)
    eye = (
        lax.broadcasted_iota(jnp.int32, (count, count), 0)
        == lax.broadcasted_iota(jnp.int32, (count, count), 1)
    ).astype(F32).astype(BF16)
    turned = lax.dot_general(eye, hot, NT, preferred_element_type=F32)
    earlier = (
        lax.broadcasted_iota(jnp.int32, (npairs, npairs), 0)
        < lax.broadcasted_iota(jnp.int32, (npairs, npairs), 1)
    ).astype(F32).astype(BF16)
    before = jnp.dot(turned.astype(BF16), earlier, preferred_element_type=F32)
    device = lax.broadcasted_iota(jnp.int32, (count, npairs), 0).astype(F32)
    slot[...] = jnp.sum(turned * (device * cap + before), axis=0, keepdims=True).astype(jnp.int32)
    wanted = turned * (remote[...] + 1).astype(F32)
    column = lax.broadcasted_iota(jnp.int32, (count, 128), 1)
    out = jnp.zeros((count, 128), F32)
    for r in range(cap):
        named = jnp.sum(jnp.where(before == r, wanted, 0.0), axis=1, keepdims=True)
        out = jnp.where(column == r, named, out)
    request[...] = out
    pl.semaphore_wait(barrier, count - 1)

    for place in ring.others:
        to, index = ring.at(place)
        pltpu.make_async_remote_copy(
            src_ref=request.at[pl.ds(index, 1)], dst_ref=asked.at[pl.ds(me, 1)],
            send_sem=sems.at[0], recv_sem=sems.at[1], device_id=to, device_id_type=MESH,
        ).start()

    own_request = pltpu.make_async_copy(request.at[pl.ds(me, 1)], asked.at[pl.ds(me, 1)], sems.at[2])
    own_request.start()
    own_request.wait()
    rest = pltpu.make_async_remote_copy(
        src_ref=request.at[pl.ds(0, count - 1)], dst_ref=asked.at[pl.ds(0, count - 1)],
        send_sem=sems.at[0], recv_sem=sems.at[1], device_id=ring.at(ring.others[0])[0], device_id_type=MESH,
    )
    rest.wait_recv()
    table[...] = asked[...].T[:8].astype(jnp.int32)
    asked_out[...] = table[...]
    to_scalars = pltpu.make_async_copy(table, scalars, sems.at[2])
    to_scalars.start()
    to_scalars.wait()

    def gather(index):
        for r in range(cap):
            send[index, r] = own[jnp.clip(scalars[r, index] - 1, 0, own.shape[0] - 1)]

    for place in ring.others:
        to, index = ring.at(place)
        gather(index)
        pltpu.make_async_remote_copy(
            src_ref=send.at[index, :, pl.ds(0, 6)], dst_ref=recv.at[me, :, pl.ds(0, 6)],
            send_sem=sems.at[3], recv_sem=sems.at[4], device_id=to, device_id_type=MESH,
        ).start()

    gather(me)
    kept = pltpu.make_async_copy(send.at[me, :, pl.ds(0, 6)], recv.at[me, :, pl.ds(0, 6)], sems.at[2])
    kept.start()
    kept.wait()
    rest.wait_send()
    every = pltpu.make_async_remote_copy(
        src_ref=send.at[pl.ds(0, count - 1), :, pl.ds(0, 6)], dst_ref=recv.at[pl.ds(0, count - 1), :, pl.ds(0, 6)],
        send_sem=sems.at[3], recv_sem=sems.at[4], device_id=ring.at(ring.others[0])[0], device_id_type=MESH,
    )
    every.wait_recv()
    every.wait_send()


def give_kernel(ret, came, sems, *, shape):
    ring = Ring(*shape)
    count, me = ring.count, ring.me
    barrier = enter(ring)
    pl.semaphore_wait(barrier, count - 1)

    for place in ring.others:
        to, index = ring.at(place)
        pltpu.make_async_remote_copy(
            src_ref=ret.at[index, :, pl.ds(0, 6)], dst_ref=came.at[me, :, pl.ds(0, 6)],
            send_sem=sems.at[0], recv_sem=sems.at[1], device_id=to, device_id_type=MESH,
        ).start()

    kept = pltpu.make_async_copy(ret.at[me, :, pl.ds(0, 6)], came.at[me, :, pl.ds(0, 6)], sems.at[2])
    kept.start()
    kept.wait()
    every = pltpu.make_async_remote_copy(
        src_ref=ret.at[pl.ds(0, count - 1), :, pl.ds(0, 6)], dst_ref=came.at[pl.ds(0, count - 1), :, pl.ds(0, 6)],
        send_sem=sems.at[0], recv_sem=sems.at[1], device_id=ring.at(ring.others[0])[0], device_id_type=MESH,
    )
    every.wait_recv()
    every.wait_send()


def add_kernel(asked, acc, came, grad, hess, parts, *, cap):
    blocks = acc.shape[0]
    parts[...] = jnp.zeros_like(parts)

    @pl.loop(0, came.shape[0], unroll=4)
    def _(d):
        for r in range(cap):
            a = asked[r, d]
            k = jnp.where(a > 0, a - 1, blocks)
            parts[r, k] += came[d, r]

    total = acc[...]
    for r in range(cap):
        total = total + parts[r, :blocks]
    parts[0, :blocks] = total
    for c in range(3):
        grad[c] = parts[0, :blocks, c]
        hess[c] = parts[0, :blocks, 3 + c]


def on_device(positions, direction, pair_local, pair_peer, pair_remote, pair_mask, *, shape):
    npairs = pair_local.shape[0]
    nblocks, width = positions.shape[1:]
    count = shape[0] * shape[1]
    cap = max(2, 2 * npairs // count)
    V = pl.BlockSpec(memory_space=pltpu.VMEM)
    S = pl.BlockSpec(memory_space=pltpu.SMEM)
    A = pl.BlockSpec(memory_space=pl.ANY)
    DMA = pltpu.SemaphoreType.DMA
    pairs_shape = jax.ShapeDtypeStruct((count, cap, 8, width), F32)
    params = functools.partial(pltpu.CompilerParams, vmem_limit_bytes=56 * 2**20)
    recv, slot, asked = pl.pallas_call(
        functools.partial(fetch_kernel, shape=shape),
        out_shape=(
            pairs_shape,
            jax.ShapeDtypeStruct((1, npairs), jnp.int32),
            jax.ShapeDtypeStruct((8, count), jnp.int32),
        ),
        in_specs=[V, V, V, V],
        out_specs=(A, V, V),
        scratch_shapes=[
            pltpu.VMEM((nblocks, 8, width), F32),
            pltpu.VMEM((count, 128), F32),
            pltpu.VMEM((count, 128), F32),
            pltpu.VMEM((8, count), jnp.int32),
            pltpu.SMEM((8, count), jnp.int32),
            pltpu.VMEM((count, cap, 8, width), F32),
            DMA((5,)),
        ],
        compiler_params=params(collective_id=0, has_side_effects=True),
        name="fetch",
    )(pair_peer, pair_remote.reshape(1, npairs), positions, direction)
    acc, ret = pl.pallas_call(
        functools.partial(pairs_kernel, npairs=npairs),
        out_shape=(
            jax.ShapeDtypeStruct((nblocks, 8, width), F32),
            jax.ShapeDtypeStruct((count * cap, 8, width), F32),
        ),
        in_specs=[S, S, V, V, V, V],
        out_specs=(V, V),
        scratch_shapes=[
            pltpu.VMEM((nblocks, 8, width), F32),
            pltpu.VMEM((nblocks, 8, width), F32),
            pltpu.VMEM((nblocks, width, KK), BF16),
            *PAIR_BUFFERS,
        ],
        compiler_params=params(),
        name="pairs",
    )(
        pair_local, slot.reshape(npairs), positions, direction, pair_mask,
        recv.reshape(count * cap, 8, width),
    )
    came = pl.pallas_call(
        functools.partial(give_kernel, shape=shape),
        out_shape=pairs_shape,
        in_specs=[A],
        out_specs=A,
        scratch_shapes=[DMA((3,))],
        compiler_params=params(collective_id=1, has_side_effects=True),
        name="give",
    )(ret.reshape(count, cap, 8, width))
    half = jax.ShapeDtypeStruct((3, nblocks, width), F32)
    return pl.pallas_call(
        functools.partial(add_kernel, cap=cap),
        out_shape=(half, half),
        in_specs=[S, V, V],
        out_specs=(V, V),
        scratch_shapes=[pltpu.VMEM((cap, nblocks + 1, 8, width), F32)],
        compiler_params=params(),
        name="add",
    )(asked, acc, came)


def solution(mesh):
    shape = (mesh.shape["dom"], mesh.shape["brick"])
    rows_of = P(None, AXES, None)
    return jax.shard_map(
        functools.partial(on_device, shape=shape),
        mesh=mesh,
        in_specs=(rows_of, rows_of, P(AXES), P(AXES, None), P(AXES), P(AXES, None)),
        out_specs=(rows_of, rows_of),
        check_vma=False,
    )
```

```python
import functools
import itertools
import math

import jax
import jax.numpy as jnp
import numpy as np
from jax import lax
from jax.experimental import pallas as pl
from jax.experimental.pallas import tpu as pltpu
from jax.sharding import PartitionSpec as P

F32, BF16 = jnp.float32, jnp.bfloat16
MESH = pl.DeviceIdType.MESH
AXES = ("dom", "brick")
NT = (((1,), (1,)), ((), ()))
K1, K2 = -0.01, 0.02
DEPTH = 80
GROUP = 8
TURNS = 4


class Places:
    def __init__(self, doms, bricks, groups):
        side = math.isqrt(bricks // 2)
        self.doms, self.bricks, self.side = doms, bricks, side
        self.count = doms * bricks
        self.sizes = (doms, side, side)
        spots = sorted(itertools.product(*map(range, self.sizes)), key=lambda s: (-self.hops(s), -len(set(s)), s))
        pairs = [s for s in spots if self.minus(s) != s and s < self.minus(s)]
        self.seeds = pairs[: 2 * groups // TURNS]
        self.list = [self.turn(h, s) for h in range(TURNS) for s in self.seeds]
        used = set(self.list)
        rest = [(*s, c) for s in spots for c in range(2) if (*s, c) not in used]
        self.list += [p for p in rest if any(p)] + [(0, 0, 0, 0)]
        self.index = {p: t for t, p in enumerate(self.list)}

    def hops(self, spot):
        return sum(min(v, n - v) for v, n in zip(spot, self.sizes))

    def minus(self, spot):
        return tuple(-v % n for v, n in zip(spot, self.sizes))

    def turn(self, h, spot):
        return (*(self.minus(spot) if h >= 2 else spot), h % 2)

    def back(self, t):
        *spot, c = self.list[t]
        return self.index[(*self.minus(spot), c)]

    def codes(self):
        return np.array([[((x * self.side + z) * self.side + y) * 2 + c] for x, y, z, c in self.list], np.int32)


class Here:
    def __init__(self, places):
        self.places = places
        side = places.side
        brick = lax.axis_index("brick")
        self.x, self.c = lax.axis_index("dom"), brick % 2
        self.y, self.z = (brick // 2) % side, brick // (2 * side)

    def coords(self, x, y, z, c):
        side = self.places.side
        brick = ((self.z + z) % side) * (2 * side) + ((self.y + y) % side) * 2 + (self.c + c) % 2
        return (self.x + x) % self.places.doms, brick

    def at(self, t):
        return self.coords(*self.places.list[t])

    def in_turn(self, h, i):
        sign = 1 + 2 * (h // 2)
        x, y, z = self.places.seeds[i]
        return self.coords(sign * x, sign * y, sign * z, h % 2)


def rows(values):
    it = lax.broadcasted_iota(jnp.int32, (8, 128), 0)
    out = jnp.zeros((8, 128), F32)
    for k, v in enumerate(values):
        if v != 0.0:
            out = jnp.where(it == k, F32(v), out)
    return out


def split3(z):
    h = z.astype(BF16).astype(F32)
    r = z - h
    m = r.astype(BF16).astype(F32)
    return h, m, r - m


def split2(z):
    h = z.astype(BF16)
    return h, (z - h.astype(F32)).astype(BF16)


def upper(n, strict_lower=False):
    a = lax.broadcasted_iota(jnp.int32, (n, n), 0)
    b = lax.broadcasted_iota(jnp.int32, (n, n), 1)
    return ((a > b) if strict_lower else (a < b)).astype(F32).astype(BF16)


def dot(a, b):
    return jnp.dot(a, b, preferred_element_type=F32)


def main_kernel(
    codes, lists, pos, dirn, mask,
    came, left, asked_out, order_out,
    own, f8, lhs, request, asked, order, table, order_s, table_s, send, recv, right, give,
    sq0, sq1, cs0, cs1, ws0, ws1, sems, *, places,
):
    here = Here(places)
    count = places.count
    cap = send.shape[0] // count
    npairs, nb = mask.shape[0], pos.shape[1]
    groups = npairs // GROUP
    self_t = count - 1
    barrier = pltpu.get_barrier_semaphore()
    for t in range(self_t):
        pl.semaphore_signal(barrier, inc=1, device_id=here.at(t), device_id_type=MESH)

    x = [pos[c] - 0.5 for c in range(3)]
    u = [dirn[c] for c in range(3)]
    a = x[0] * x[0] + x[1] * x[1] + x[2] * x[2] + 0.1
    b = x[0] * u[0] + x[1] * u[1] + x[2] * u[2]
    for k, v in enumerate(x + u + [jnp.ones_like(a), jnp.zeros_like(a)]):
        own[:, k, :] = v
    for k, v in enumerate(x + [a, b] + u):
        f8[:, k, :] = v

    peer = lists[0:1, :]
    remote = lists[1:2, :].astype(F32)
    local = lists[2:3, :].astype(F32)
    side = places.side
    cx = codes[...] // (2 * side * side)
    cz = (codes[...] // (2 * side)) % side
    cy = (codes[...] // 2) % side
    cc = codes[...] % 2
    device = (
        ((here.x + cx) % places.doms) * places.bricks
        + ((here.z + cz) % side) * (2 * side) + ((here.y + cy) % side) * 2 + (here.c + cc) % 2
    )
    hot = jnp.where(device == peer, 1.0, 0.0)
    hot16 = hot.astype(BF16)
    before = dot(hot16, upper(npairs))
    base = jnp.sum(dot(upper(count, True), hot16), axis=1, keepdims=True)
    place = lax.broadcasted_iota(jnp.int32, (count, npairs), 0).astype(F32)
    rank = jnp.sum(hot * before, axis=0, keepdims=True)
    where_t = jnp.sum(hot * place, axis=0, keepdims=True)
    sorted_k = jnp.sum(hot * (before + base), axis=0, keepdims=True)
    it256 = lax.broadcasted_iota(jnp.int32, (npairs, npairs), 0).astype(F32)
    moved = jnp.where(it256 == sorted_k, 1.0, 0.0).astype(BF16)
    number = lax.broadcasted_iota(jnp.int32, (1, npairs), 1).astype(F32)
    sub = lax.broadcasted_iota(jnp.int32, (8, npairs), 0)
    values = jnp.zeros((8, npairs), F32)
    for k, v in enumerate([where_t, rank, local, number]):
        values = jnp.where(sub == k, v, values)
    values = lax.dot_general(values.astype(BF16), moved, NT, preferred_element_type=F32)
    values = jnp.where(sub == 1, values[1:2] + cap * values[0:1], values)
    order[...] = values.astype(jnp.int32)
    wanted = hot * (remote + 1.0)
    lane = lax.broadcasted_iota(jnp.int32, (count, 128), 1)
    out = jnp.where(lane == cap, base, 0.0)
    for r in range(cap):
        named = jnp.sum(jnp.where(before == r, wanted, 0.0), axis=1, keepdims=True)
        out = jnp.where(lane == r, named, out)
    request[...] = out
    order_out[...] = order[...]
    to_order = pltpu.make_async_copy(order, order_s, sems.at[2])
    to_order.start()

    pl.semaphore_wait(barrier, count - 1)
    for t in range(self_t):
        pltpu.make_async_remote_copy(
            src_ref=request.at[pl.ds(t, 1)], dst_ref=asked.at[pl.ds(places.back(t), 1)],
            send_sem=sems.at[0], recv_sem=sems.at[1], device_id=here.at(t), device_id_type=MESH,
        ).start()

    eye = (
        lax.broadcasted_iota(jnp.int32, (128, 128), 0) == lax.broadcasted_iota(jnp.int32, (128, 128), 1)
    ).astype(F32).astype(BF16)
    ones3 = rows([1, 1, 1])
    zero = jnp.zeros((8, 128), F32)

    @pl.loop(0, nb // 8)
    def _(g):
        for j in range(8):
            k = g * 8 + j
            h, m, l = split3(f8[k])
            fk = jnp.concatenate([h, h, m, m, h, l, ones3, ones3, ones3, zero], axis=0).astype(BF16)
            lhs[k] = lax.dot_general(eye, fk, NT, preferred_element_type=F32).astype(BF16)

    right[pl.ds(npairs, 8)] = jnp.zeros((8, 8, 128), F32)
    cs1[...] = jnp.zeros_like(cs1)
    ws1[...] = jnp.zeros_like(ws1)
    to_order.wait()
    rest = pltpu.make_async_remote_copy(
        src_ref=request.at[pl.ds(0, self_t)], dst_ref=asked.at[pl.ds(0, self_t)],
        send_sem=sems.at[0], recv_sem=sems.at[1], device_id=here.at(0), device_id_type=MESH,
    )
    rest.wait_recv()
    at_place = lax.broadcasted_iota(jnp.int32, (count, 128), 0)
    both = jnp.where(at_place == self_t, request[...], jnp.where(at_place < self_t, asked[...], 0.0)).T
    bases = request[...].T
    sub8 = lax.broadcasted_iota(jnp.int32, (8, count), 0)
    table[...] = jnp.where(sub8 < cap, both[:8], bases[:8]).astype(jnp.int32)
    asked_out[...] = table[...]
    to_scalars = pltpu.make_async_copy(table, table_s, sems.at[2])
    to_scalars.start()
    to_scalars.wait()

    def slots(t):
        return pl.ds(cap * t, cap)

    for t in range(count):
        for r in range(cap):
            send[cap * t + r] = own[jnp.clip(table_s[r, t] - 1, 0, nb - 1)]
        if t < self_t:
            pltpu.make_async_remote_copy(
                src_ref=send.at[slots(t), pl.ds(0, 6)], dst_ref=recv.at[slots(places.back(t)), pl.ds(0, 6)],
                send_sem=sems.at[3], recv_sem=sems.at[4], device_id=here.at(t), device_id_type=MESH,
            ).start()
    kept = pltpu.make_async_copy(
        send.at[slots(self_t), pl.ds(0, 6)], recv.at[slots(self_t), pl.ds(0, 6)], sems.at[2]
    )
    kept.start()
    kept.wait()
    rest.wait_send()
    every = pltpu.make_async_remote_copy(
        src_ref=send.at[pl.ds(0, cap * self_t), pl.ds(0, 6)], dst_ref=recv.at[pl.ds(0, cap * self_t), pl.ds(0, 6)],
        send_sem=sems.at[3], recv_sem=sems.at[4], device_id=here.at(0), device_id_type=MESH,
    )
    every.wait_recv()

    it = lax.broadcasted_iota(jnp.int32, (8, 128), 0)
    lane128 = lax.broadcasted_iota(jnp.int32, (128, 128), 1)
    top = rows([0, 0, 0, 0, 0, 0, 1])
    cp = rows([-2, -2, -2])
    e3 = rows([0, 0, 0, 1])
    e34 = rows([0, 0, 0, 1, 1])
    last = rows([0, 0, 0, 0, 0, 0, 0, 1])
    m35 = rows([0, 0, 0, 1, 1, 1])
    sq, cs, ws = (sq0, sq1), (cs0, cs1), (ws0, ws1)

    def whole(row):
        return jnp.broadcast_to(row, (8, 128))

    def spread(z):
        h, m, l = split3(z)
        return [h, m, h, m, l, h]

    def halves(z):
        h, l, _ = split3(z)
        return jnp.concatenate([h, l], axis=0).astype(BF16)

    def block(p):
        return jnp.clip(order_s[2, p], 0, nb - 1)

    def other(p):
        return jnp.where(it < 6, recv[jnp.clip(order_s[1, p], 0, cap * count - 1)], top)

    def active(p):
        return whole(mask[pl.ds(jnp.clip(order_s[3, p], 0, npairs - 1), 1), :].astype(F32))

    def distances(p, j, out):
        b = other(p)
        ro = pltpu.roll(b, 5, 0)
        rp = jnp.concatenate(spread(b * cp + e3) + list(split3(b * b)) + [zero], axis=0).astype(BF16)
        rq = jnp.concatenate(spread(e34 - ro) + list(split3(b * ro)) + [zero], axis=0).astype(BF16)
        out[pl.ds(128 * j, 128), :] = dot(lhs[block(p)], jnp.concatenate([rp, rq], axis=1))

    def factors(p, j, given, c, w):
        b = other(p)
        rs = pl.ds(128 * j, 128)
        s = jnp.minimum(given[rs, 0:128], 1.0)
        l2 = 2.0 * jnp.log(s)
        t = 1.0 - 1.0 / s
        c1h, c1l = split2((s - 1.0) * (l2 + t))
        c2h, c2l = split2((t * (t - 4.0) - l2) * given[rs, 128:256])
        c[pl.ds(256 * j, 128), 0:128] = c1h
        c[pl.ds(256 * j, 128), 128:256] = c2h
        c[pl.ds(256 * j + 128, 128), 0:128] = c1l
        c[pl.ds(256 * j + 128, 128), 128:256] = c2l
        x = halves(own[block(p)] * active(p))
        r = dot(jnp.concatenate([x, x], axis=1), c[pl.ds(256 * j, 256), :])
        r = r[:8] + r[8:]
        r1, r2 = r[:, :128], r[:, 128:]
        d1 = r1 - b * whole(r1[6:7])
        d2 = r2 - b * whole(r2[6:7])
        right[p] = (-K1) * d1 - K2 * m35 * pltpu.roll(d2, 3, 0)
        w[pl.ds(16 * j, 16), 0:128] = halves(K1 * b)
        w[pl.ds(16 * j, 16), 128:256] = halves(K2 * (m35 * pltpu.roll(b, 3, 0) + last))

    def residents(g, c, w):
        res = lax.dot_general(c[...], w[...], NT, preferred_element_type=F32)
        tot = res[:128] + res[128:256]
        for j in range(1, GROUP):
            tot = jnp.where(
                lane128 >= 16 * j, res[256 * j : 256 * j + 128] + res[256 * j + 128 : 256 * j + 256], tot
            )
        tr = tot.T
        for j in range(GROUP):
            p = g * GROUP + j
            o = own[block(p)]
            sums = tr[16 * j : 16 * j + 8] + tr[16 * j + 8 : 16 * j + 16]
            term = o * whole(sums[6:7]) + m35 * pltpu.roll(o, 3, 0) * whole(sums[7:8]) - sums
            left[p] = active(p) * term

    def hand_back(t, back, to):
        first = jnp.clip(table_s[cap, t], 0, npairs)
        for r in range(cap):
            give[cap * t + r] = right[first + r]
        return pltpu.make_async_remote_copy(
            src_ref=give.at[slots(t), pl.ds(0, 6)], dst_ref=came.at[slots(back), pl.ds(0, 6)],
            send_sem=sems.at[5], recv_sem=sems.at[6], device_id=to, device_id_type=MESH,
        ).start()

    per_turn = groups // TURNS
    for j in range(GROUP):
        distances(j, j, sq0)

    @pl.loop(0, TURNS)
    def _(h):
        for k in range(per_turn):
            odd = k % 2
            g = per_turn * h + k
            after = jnp.minimum(g + 1, groups - 1) if k == per_turn - 1 else g + 1
            residents(jnp.maximum(g - 1, 0) if k == 0 else g - 1, cs[1 - odd], ws[1 - odd])
            for j in range(GROUP):
                distances(after * GROUP + j, j, sq[1 - odd])
                factors(g * GROUP + j, j, sq[odd], cs[odd], ws[odd])
            for i in (2 * k, 2 * k + 1):
                hand_back(h * 2 * per_turn + i, ((h + 2) % TURNS) * 2 * per_turn + i, here.in_turn(h, i))

    for t in range(2 * groups, self_t):
        hand_back(t, places.back(t), here.at(t))
    first = jnp.clip(table_s[cap, self_t], 0, npairs)
    for r in range(cap):
        give[cap * self_t + r] = right[first + r]
    kept = pltpu.make_async_copy(
        give.at[slots(self_t), pl.ds(0, 6)], came.at[slots(self_t), pl.ds(0, 6)], sems.at[2]
    )
    kept.start()
    residents(groups - 1, cs1, ws1)
    kept.wait()
    every.wait_send()
    final = pltpu.make_async_remote_copy(
        src_ref=give.at[pl.ds(0, cap * self_t), pl.ds(0, 6)], dst_ref=came.at[pl.ds(0, cap * self_t), pl.ds(0, 6)],
        send_sem=sems.at[5], recv_sem=sems.at[6], device_id=here.at(0), device_id_type=MESH,
    )
    final.wait_recv()
    final.wait_send()


def add_kernel(asked, order, left, came, grad, hess, parts, *, cap):
    chains, blocks = parts.shape[0], parts.shape[1] - 1
    parts[...] = jnp.zeros_like(parts)

    @pl.loop(0, left.shape[0] // chains, unroll=2)
    def _(g):
        for r in range(chains):
            p = g * chains + r
            parts[r, order[2, p]] += left[p]

    @pl.loop(0, came.shape[0] // cap, unroll=4)
    def _(d):
        for r in range(cap):
            a = asked[r, d]
            k = jnp.where(a > 0, a - 1, blocks)
            parts[r, k] += came[cap * d + r]

    total = parts[0, :blocks]
    for r in range(1, chains):
        total = total + parts[r, :blocks]
    parts[0, :blocks] = total
    for c in range(3):
        grad[c] = parts[0, :blocks, c]
        hess[c] = parts[0, :blocks, 3 + c]


def on_device(positions, direction, pair_local, pair_peer, pair_remote, pair_mask, *, shape):
    npairs = pair_local.shape[0]
    nb, width = positions.shape[1:]
    places = Places(*shape, npairs // GROUP)
    count = places.count
    cap = max(2, 2 * npairs // count)
    V = pl.BlockSpec(memory_space=pltpu.VMEM)
    S = pl.BlockSpec(memory_space=pltpu.SMEM)
    A = pl.BlockSpec(memory_space=pl.ANY)
    params = functools.partial(pltpu.CompilerParams, vmem_limit_bytes=60 * 2**20)
    tiles = lambda n: pltpu.VMEM((n, 8, width), F32)
    lists = jnp.stack([pair_peer[:, 0], pair_remote, pair_local])
    came, left, asked, order = pl.pallas_call(
        functools.partial(main_kernel, places=places),
        out_shape=(
            jax.ShapeDtypeStruct((count * cap, 8, width), F32),
            jax.ShapeDtypeStruct((npairs, 8, width), F32),
            jax.ShapeDtypeStruct((8, count), jnp.int32),
            jax.ShapeDtypeStruct((8, npairs), jnp.int32),
        ),
        in_specs=[V] * 5,
        out_specs=(A, V, V, V),
        scratch_shapes=[
            tiles(nb), tiles(nb), pltpu.VMEM((nb, width, DEPTH), BF16),
            pltpu.VMEM((count, 128), F32), pltpu.VMEM((count, 128), F32),
            pltpu.VMEM((8, npairs), jnp.int32), pltpu.VMEM((8, count), jnp.int32),
            pltpu.SMEM((8, npairs), jnp.int32), pltpu.SMEM((8, count), jnp.int32),
            tiles(count * cap), tiles(count * cap), tiles(npairs + 8), tiles(count * cap),
            *[pltpu.VMEM((128 * GROUP, 256), F32)] * 2,
            *[pltpu.VMEM((256 * GROUP, 256), BF16)] * 2,
            *[pltpu.VMEM((16 * GROUP, 256), BF16)] * 2,
            pltpu.SemaphoreType.DMA((7,)),
        ],
        compiler_params=params(collective_id=0, has_side_effects=True),
        name="main",
    )(places.codes(), lists, positions, direction, pair_mask)
    half = jax.ShapeDtypeStruct((3, nb, width), F32)
    return pl.pallas_call(
        functools.partial(add_kernel, cap=cap),
        out_shape=(half, half),
        in_specs=[S, S, V, V],
        out_specs=(V, V),
        scratch_shapes=[pltpu.VMEM((cap, nb + 1, 8, width), F32)],
        compiler_params=params(),
        name="add",
    )(asked, order, left, came)


def solution(mesh):
    shape = (mesh.shape["dom"], mesh.shape["brick"])
    rows_of = P(None, AXES, None)
    return jax.shard_map(
        functools.partial(on_device, shape=shape),
        mesh=mesh,
        in_specs=(rows_of, rows_of, P(AXES), P(AXES, None), P(AXES), P(AXES, None)),
        out_specs=(rows_of, rows_of),
        check_vma=False,
    )
```

```python
import functools
import itertools
import math

import jax
import jax.numpy as jnp
import numpy as np
from jax import lax
from jax.experimental import pallas as pl
from jax.experimental.pallas import tpu as pltpu
from jax.sharding import PartitionSpec as P

F32, BF16 = jnp.float32, jnp.bfloat16
MESH = pl.DeviceIdType.MESH
AXES = ("dom", "brick")
NT = (((1,), (1,)), ((), ()))
K1, K2 = -0.01, 0.02
DEPTH = 80
GROUP = 8
TURNS = 4


class Places:
    def __init__(self, doms, bricks, groups):
        side = math.isqrt(bricks // 2)
        self.doms, self.bricks, self.side = doms, bricks, side
        self.count = doms * bricks
        self.sizes = (doms, side, side)
        spots = sorted(itertools.product(*map(range, self.sizes)), key=lambda s: (-self.hops(s), -len(set(s)), s))
        pairs = [s for s in spots if self.minus(s) != s and s < self.minus(s)]
        self.seeds = pairs[: 2 * groups // TURNS]
        self.list = [self.turn(h, i) for h in range(TURNS) for i in range(len(self.seeds))]
        used = set(self.list)
        rest = [(*s, c) for s in spots for c in range(2) if (*s, c) not in used]
        self.list += [p for p in rest if any(p)] + [(0, 0, 0, 0)]
        self.index = {p: t for t, p in enumerate(self.list)}

    def hops(self, spot):
        return sum(min(v, n - v) for v, n in zip(spot, self.sizes))

    def minus(self, spot):
        return tuple(-v % n for v, n in zip(spot, self.sizes))

    def turn(self, h, i):
        spot = self.seeds[i]
        return (*(self.minus(spot) if (h // 2 + i) % 2 else spot), h % 2)

    def back(self, t):
        *spot, c = self.list[t]
        return self.index[(*self.minus(spot), c)]

    def codes(self):
        return np.array([[((x * self.side + z) * self.side + y) * 2 + c] for x, y, z, c in self.list], np.int32)


class Here:
    def __init__(self, places):
        self.places = places
        side = places.side
        brick = lax.axis_index("brick")
        self.x, self.c = lax.axis_index("dom"), brick % 2
        self.y, self.z = (brick // 2) % side, brick // (2 * side)
        self.xs = [(self.x + k) % places.doms for k in range(places.doms)]
        self.ys = [((self.y + k) % side) * 2 for k in range(side)]
        self.zs = [((self.z + k) % side) * (2 * side) for k in range(side)]
        self.cs = [(self.c + k) % 2 for k in range(2)]

    def coords(self, x, y, z, c):
        side = self.places.side
        brick = ((self.z + z) % side) * (2 * side) + ((self.y + y) % side) * 2 + (self.c + c) % 2
        return (self.x + x) % self.places.doms, brick

    def at(self, t):
        x, y, z, c = self.places.list[t]
        return self.xs[x], self.zs[z] + self.ys[y] + self.cs[c]

    def in_turn(self, h, i):
        sign = 1 + 2 * ((h // 2 + i) % 2)
        x, y, z = self.places.seeds[i]
        return self.coords(sign * x, sign * y, sign * z, h % 2)


def rows(values):
    it = lax.broadcasted_iota(jnp.int32, (8, 128), 0)
    out = jnp.zeros((8, 128), F32)
    for k, v in enumerate(values):
        if v != 0.0:
            out = jnp.where(it == k, F32(v), out)
    return out


def split3(z):
    h = z.astype(BF16).astype(F32)
    r = z - h
    m = r.astype(BF16).astype(F32)
    return h, m, r - m


def split2(z):
    h = z.astype(BF16)
    return h, (z - h.astype(F32)).astype(BF16)


def upper(n, strict_lower=False):
    a = lax.broadcasted_iota(jnp.int32, (n, n), 0)
    b = lax.broadcasted_iota(jnp.int32, (n, n), 1)
    return ((a > b) if strict_lower else (a < b)).astype(F32).astype(BF16)


def dot(a, b):
    return jnp.dot(a, b, preferred_element_type=F32)


def main_kernel(
    codes, peers, remotes, locals_, pos, dirn, mask,
    came, sums_out, asked_out,
    own, f8, lhs, request, asked, order, table, order_s, table_s, send, recv, right, left, give,
    sq0, sq1, cs0, cs1, ws0, ws1, sems, *, places,
):
    here = Here(places)
    count = places.count
    cap = send.shape[0] // count
    npairs, nb = mask.shape[0], pos.shape[1]
    groups = npairs // GROUP
    self_t = count - 1
    barrier = pltpu.get_barrier_semaphore()
    for t in range(self_t):
        pl.semaphore_signal(barrier, inc=1, device_id=here.at(t), device_id_type=MESH)

    x = [pos[c] - 0.5 for c in range(3)]
    u = [dirn[c] for c in range(3)]
    a = x[0] * x[0] + x[1] * x[1] + x[2] * x[2] + 0.1
    b = x[0] * u[0] + x[1] * u[1] + x[2] * u[2]
    for k, v in enumerate(x + u + [jnp.ones_like(a), jnp.zeros_like(a)]):
        own[:, k, :] = v
    for k, v in enumerate(x + [a, b] + u):
        f8[:, k, :] = v

    peer = peers[...]
    remote = remotes[...].astype(F32)
    local = locals_[...].astype(F32)
    side = places.side
    cx = codes[...] // (2 * side * side)
    cz = (codes[...] // (2 * side)) % side
    cy = (codes[...] // 2) % side
    cc = codes[...] % 2
    device = (
        ((here.x + cx) % places.doms) * places.bricks
        + ((here.z + cz) % side) * (2 * side) + ((here.y + cy) % side) * 2 + (here.c + cc) % 2
    )
    hot = jnp.where(device == peer, 1.0, 0.0)
    hot16 = hot.astype(BF16)
    before = dot(hot16, upper(npairs))
    base = jnp.sum(dot(upper(count, True), hot16), axis=1, keepdims=True)
    place = lax.broadcasted_iota(jnp.int32, (count, npairs), 0).astype(F32)
    rank = jnp.sum(hot * before, axis=0, keepdims=True)
    where_t = jnp.sum(hot * place, axis=0, keepdims=True)
    sorted_k = jnp.sum(hot * (before + base), axis=0, keepdims=True)
    it256 = lax.broadcasted_iota(jnp.int32, (npairs, npairs), 0).astype(F32)
    moved = jnp.where(it256 == sorted_k, 1.0, 0.0).astype(BF16)
    number = lax.broadcasted_iota(jnp.int32, (1, npairs), 1).astype(F32)
    sub = lax.broadcasted_iota(jnp.int32, (8, npairs), 0)
    values = jnp.zeros((8, npairs), F32)
    for k, v in enumerate([where_t, rank, local, number]):
        values = jnp.where(sub == k, v, values)
    values = lax.dot_general(values.astype(BF16), moved, NT, preferred_element_type=F32)
    values = jnp.where(sub == 1, values[1:2] + cap * values[0:1], values)
    order[...] = values.astype(jnp.int32)
    wanted = hot * (remote + 1.0)
    lane = lax.broadcasted_iota(jnp.int32, (count, 128), 1)
    out = jnp.where(lane == cap, base, 0.0)
    for r in range(cap):
        named = jnp.sum(jnp.where(before == r, wanted, 0.0), axis=1, keepdims=True)
        out = jnp.where(lane == r, named, out)
    request[...] = out
    to_order = pltpu.make_async_copy(order, order_s, sems.at[2])
    to_order.start()

    pl.semaphore_wait(barrier, count - 1)
    for t in range(self_t):
        pltpu.make_async_remote_copy(
            src_ref=request.at[pl.ds(t, 1)], dst_ref=asked.at[pl.ds(places.back(t), 1)],
            send_sem=sems.at[0], recv_sem=sems.at[1], device_id=here.at(t), device_id_type=MESH,
        ).start()

    eye = (
        lax.broadcasted_iota(jnp.int32, (128, 128), 0) == lax.broadcasted_iota(jnp.int32, (128, 128), 1)
    ).astype(F32).astype(BF16)
    ones3 = rows([1, 1, 1])
    zero = jnp.zeros((8, 128), F32)

    @pl.loop(0, nb // 8)
    def _(g):
        for j in range(8):
            k = g * 8 + j
            h, m, l = split3(f8[k])
            fk = jnp.concatenate([h, h, m, m, h, l, ones3, ones3, ones3, zero], axis=0).astype(BF16)
            lhs[k] = lax.dot_general(eye, fk, NT, preferred_element_type=F32).astype(BF16)

    right[pl.ds(npairs, 8)] = jnp.zeros((8, 8, 128), F32)
    cs1[...] = jnp.zeros_like(cs1)
    ws1[...] = jnp.zeros_like(ws1)
    to_order.wait()
    rest = pltpu.make_async_remote_copy(
        src_ref=request.at[pl.ds(0, self_t)], dst_ref=asked.at[pl.ds(0, self_t)],
        send_sem=sems.at[0], recv_sem=sems.at[1], device_id=here.at(0), device_id_type=MESH,
    )
    rest.wait_recv()
    at_place = lax.broadcasted_iota(jnp.int32, (count, 128), 0)
    both = jnp.where(at_place == self_t, request[...], jnp.where(at_place < self_t, asked[...], 0.0)).T
    bases = request[...].T
    sub8 = lax.broadcasted_iota(jnp.int32, (8, count), 0)
    table[...] = jnp.where(sub8 < cap, both[:8], bases[:8]).astype(jnp.int32)
    asked_out[...] = table[...]
    to_scalars = pltpu.make_async_copy(table, table_s, sems.at[2])
    to_scalars.start()
    to_scalars.wait()

    def slots(t):
        return pl.ds(cap * t, cap)

    for t in range(count):
        for r in range(cap):
            send[cap * t + r] = own[jnp.clip(table_s[r, t] - 1, 0, nb - 1)]
        if t < self_t:
            pltpu.make_async_remote_copy(
                src_ref=send.at[slots(t), pl.ds(0, 6)], dst_ref=recv.at[slots(places.back(t)), pl.ds(0, 6)],
                send_sem=sems.at[3], recv_sem=sems.at[4], device_id=here.at(t), device_id_type=MESH,
            ).start()
    kept = pltpu.make_async_copy(
        send.at[slots(self_t), pl.ds(0, 6)], recv.at[slots(self_t), pl.ds(0, 6)], sems.at[2]
    )
    kept.start()
    kept.wait()
    rest.wait_send()
    every = pltpu.make_async_remote_copy(
        src_ref=send.at[pl.ds(0, cap * self_t), pl.ds(0, 6)], dst_ref=recv.at[pl.ds(0, cap * self_t), pl.ds(0, 6)],
        send_sem=sems.at[3], recv_sem=sems.at[4], device_id=here.at(0), device_id_type=MESH,
    )
    every.wait_recv()

    it = lax.broadcasted_iota(jnp.int32, (8, 128), 0)
    lane128 = lax.broadcasted_iota(jnp.int32, (128, 128), 1)
    top = rows([0, 0, 0, 0, 0, 0, 1])
    cp = rows([-2, -2, -2])
    e3 = rows([0, 0, 0, 1])
    e34 = rows([0, 0, 0, 1, 1])
    last = rows([0, 0, 0, 0, 0, 0, 0, 1])
    m35 = rows([0, 0, 0, 1, 1, 1])
    sq, cs, ws = (sq0, sq1), (cs0, cs1), (ws0, ws1)

    def whole(row):
        return jnp.broadcast_to(row, (8, 128))

    def spread(z):
        h, m, l = split3(z)
        return [h, m, h, m, l, h]

    def halves(z):
        h, l, _ = split3(z)
        return jnp.concatenate([h, l], axis=0).astype(BF16)

    def block(p):
        return jnp.clip(order_s[2, p], 0, nb - 1)

    def other(p):
        return jnp.where(it < 6, recv[jnp.clip(order_s[1, p], 0, cap * count - 1)], top)

    def active(p):
        return whole(mask[pl.ds(jnp.clip(order_s[3, p], 0, npairs - 1), 1), :].astype(F32))

    def distances(p, j, out):
        b = other(p)
        ro = pltpu.roll(b, 5, 0)
        rp = jnp.concatenate(spread(b * cp + e3) + list(split3(b * b)) + [zero], axis=0).astype(BF16)
        rq = jnp.concatenate(spread(e34 - ro) + list(split3(b * ro)) + [zero], axis=0).astype(BF16)
        out[pl.ds(128 * j, 128), :] = dot(lhs[block(p)], jnp.concatenate([rp, rq], axis=1))

    def factors(p, j, given, c, w):
        b = other(p)
        rs = pl.ds(128 * j, 128)
        s = jnp.minimum(given[rs, 0:128], 1.0)
        l2 = 2.0 * jnp.log(s)
        t = 1.0 - 1.0 / s
        c1h, c1l = split2((s - 1.0) * (l2 + t))
        c2h, c2l = split2((t * (t - 4.0) - l2) * given[rs, 128:256])
        c[pl.ds(256 * j, 128), 0:128] = c1h
        c[pl.ds(256 * j, 128), 128:256] = c2h
        c[pl.ds(256 * j + 128, 128), 0:128] = c1l
        c[pl.ds(256 * j + 128, 128), 128:256] = c2l
        x = halves(own[block(p)] * active(p))
        r = dot(jnp.concatenate([x, x], axis=1), c[pl.ds(256 * j, 256), :])
        r = r[:8] + r[8:]
        r1, r2 = r[:, :128], r[:, 128:]
        d1 = r1 - b * whole(r1[6:7])
        d2 = r2 - b * whole(r2[6:7])
        right[p] = (-K1) * d1 - K2 * m35 * pltpu.roll(d2, 3, 0)
        w[pl.ds(16 * j, 16), 0:128] = halves(K1 * b)
        w[pl.ds(16 * j, 16), 128:256] = halves(K2 * (m35 * pltpu.roll(b, 3, 0) + last))

    def residents(g, c, w):
        res = lax.dot_general(c[...], w[...], NT, preferred_element_type=F32)
        tot = res[:128] + res[128:256]
        for j in range(1, GROUP):
            tot = jnp.where(
                lane128 >= 16 * j, res[256 * j : 256 * j + 128] + res[256 * j + 128 : 256 * j + 256], tot
            )
        tr = tot.T
        for j in range(GROUP):
            p = g * GROUP + j
            o = own[block(p)]
            sums = tr[16 * j : 16 * j + 8] + tr[16 * j + 8 : 16 * j + 16]
            term = o * whole(sums[6:7]) + m35 * pltpu.roll(o, 3, 0) * whole(sums[7:8]) - sums
            left[p] = active(p) * term

    def hand_back(t, back, to):
        first = jnp.clip(table_s[cap, t], 0, npairs)
        for r in range(cap):
            give[cap * t + r] = right[first + r]
        return pltpu.make_async_remote_copy(
            src_ref=give.at[slots(t), pl.ds(0, 6)], dst_ref=came.at[slots(back), pl.ds(0, 6)],
            send_sem=sems.at[5], recv_sem=sems.at[6], device_id=to, device_id_type=MESH,
        ).start()

    per_turn = groups // TURNS
    for j in range(GROUP):
        distances(j, j, sq0)

    @pl.loop(0, TURNS)
    def _(h):
        for k in range(per_turn):
            odd = k % 2
            g = per_turn * h + k
            after = jnp.minimum(g + 1, groups - 1) if k == per_turn - 1 else g + 1
            residents(jnp.maximum(g - 1, 0) if k == 0 else g - 1, cs[1 - odd], ws[1 - odd])
            for j in range(GROUP):
                distances(after * GROUP + j, j, sq[1 - odd])
                factors(g * GROUP + j, j, sq[odd], cs[odd], ws[odd])
        for i in range(2 * per_turn):
            hand_back(h * 2 * per_turn + i, ((h + 2) % TURNS) * 2 * per_turn + i, here.in_turn(h, i))

    for t in range(2 * groups, self_t):
        hand_back(t, places.back(t), here.at(t))
    first = jnp.clip(table_s[cap, self_t], 0, npairs)
    for r in range(cap):
        give[cap * self_t + r] = right[first + r]
    kept = pltpu.make_async_copy(
        give.at[slots(self_t), pl.ds(0, 6)], came.at[slots(self_t), pl.ds(0, 6)], sems.at[2]
    )
    kept.start()
    residents(groups - 1, cs1, ws1)
    block_of = lax.broadcasted_iota(jnp.int32, (nb, npairs), 0)
    chosen = jnp.where(block_of == order[2:3, :], 1.0, 0.0).astype(BF16)
    for c in range(6):
        parts = jnp.concatenate(split3(left[:, c, :]), axis=1).astype(BF16)
        sums = dot(chosen, parts)
        sums_out[c] = sums[:, :128] + sums[:, 128:256] + sums[:, 256:]
    kept.wait()
    every.wait_send()
    final = pltpu.make_async_remote_copy(
        src_ref=give.at[pl.ds(0, cap * self_t), pl.ds(0, 6)], dst_ref=came.at[pl.ds(0, cap * self_t), pl.ds(0, 6)],
        send_sem=sems.at[5], recv_sem=sems.at[6], device_id=here.at(0), device_id_type=MESH,
    )
    final.wait_recv()
    final.wait_send()


def add_kernel(asked, sums, came, grad, hess, *parts, cap):
    step = pl.program_id(0)
    blocks = parts[0].shape[0] - 1
    here = came.shape[0] // cap

    @pl.when(step == 0)
    def _():
        for part in parts:
            part[...] = jnp.zeros_like(part)

    @pl.loop(0, here // 8)
    def _(g):
        for j in range(8):
            d = g * 8 + j
            for r in range(cap):
                a = asked[r, step * here + d]
                k = jnp.where(a > 0, a - 1, blocks)
                parts[(j * cap + r) % len(parts)][k] += came[cap * d + r]

    @pl.when(step == pl.num_programs(0) - 1)
    def _():
        total = parts[0][:blocks]
        for part in parts[1:]:
            total = total + part[:blocks]
        parts[0][:blocks] = total
        for c in range(3):
            grad[c] = parts[0][:blocks, c] + sums[c]
            hess[c] = parts[0][:blocks, 3 + c] + sums[3 + c]


def on_device(positions, direction, pair_local, pair_peer, pair_remote, pair_mask, *, shape):
    npairs = pair_local.shape[0]
    nb, width = positions.shape[1:]
    places = Places(*shape, npairs // GROUP)
    count = places.count
    cap = max(2, 2 * npairs // count)
    V = pl.BlockSpec(memory_space=pltpu.VMEM)
    S = pl.BlockSpec(memory_space=pltpu.SMEM)
    A = pl.BlockSpec(memory_space=pl.ANY)
    params = functools.partial(pltpu.CompilerParams, vmem_limit_bytes=60 * 2**20)
    tiles = lambda n: pltpu.VMEM((n, 8, width), F32)
    row = lambda v: v.reshape(1, npairs)
    came, sums, asked = pl.pallas_call(
        functools.partial(main_kernel, places=places),
        out_shape=(
            jax.ShapeDtypeStruct((count * cap, 8, width), F32),
            jax.ShapeDtypeStruct((6, nb, width), F32),
            jax.ShapeDtypeStruct((8, count), jnp.int32),
        ),
        in_specs=[V] * 7,
        out_specs=(A, V, V),
        scratch_shapes=[
            tiles(nb), tiles(nb), pltpu.VMEM((nb, width, DEPTH), BF16),
            pltpu.VMEM((count, 128), F32), pltpu.VMEM((count, 128), F32),
            pltpu.VMEM((8, npairs), jnp.int32), pltpu.VMEM((8, count), jnp.int32),
            pltpu.SMEM((8, npairs), jnp.int32), pltpu.SMEM((8, count), jnp.int32),
            tiles(count * cap), tiles(count * cap), tiles(npairs + 8), tiles(npairs), tiles(count * cap),
            *[pltpu.VMEM((128 * GROUP, 256), F32)] * 2,
            *[pltpu.VMEM((256 * GROUP, 256), BF16)] * 2,
            *[pltpu.VMEM((16 * GROUP, 256), BF16)] * 2,
            pltpu.SemaphoreType.DMA((7,)),
        ],
        compiler_params=params(collective_id=0, has_side_effects=True),
        name="main",
    )(places.codes(), row(pair_peer), row(pair_remote), row(pair_local), positions, direction, pair_mask)
    half = jax.ShapeDtypeStruct((3, nb, width), F32)
    chunks = 4
    return pl.pallas_call(
        functools.partial(add_kernel, cap=cap),
        out_shape=(half, half),
        grid=(chunks,),
        in_specs=[S, V, pl.BlockSpec((count * cap // chunks, 8, width), lambda i: (i, 0, 0))],
        out_specs=(V, V),
        scratch_shapes=[tiles(nb + 1)] * 8,
        compiler_params=params(),
        name="add",
    )(asked, sums, came)


def solution(mesh):
    shape = (mesh.shape["dom"], mesh.shape["brick"])
    rows_of = P(None, AXES, None)
    return jax.shard_map(
        functools.partial(on_device, shape=shape),
        mesh=mesh,
        in_specs=(rows_of, rows_of, P(AXES), P(AXES, None), P(AXES), P(AXES, None)),
        out_specs=(rows_of, rows_of),
        check_vma=False,
    )
```

```python
import functools
import itertools
import math

import jax
import jax.numpy as jnp
import numpy as np
from jax import lax
from jax.experimental import pallas as pl
from jax.experimental.pallas import tpu as pltpu
from jax.sharding import PartitionSpec as P

F32, BF16 = jnp.float32, jnp.bfloat16
MESH = pl.DeviceIdType.MESH
AXES = ("dom", "brick")
NT = (((1,), (1,)), ((), ()))
K1, K2 = -0.01, 0.02
DEPTH = 80
GROUP = 8
TURNS = 4
AHEAD = 4


class Places:
    def __init__(self, doms, bricks, groups):
        side = math.isqrt(bricks // 2)
        self.doms, self.bricks, self.side = doms, bricks, side
        self.count = doms * bricks
        self.sizes = (doms, side, side)
        spots = sorted(itertools.product(*map(range, self.sizes)), key=lambda s: (-self.hops(s), -len(set(s)), s))
        pairs = [s for s in spots if self.minus(s) != s and s < self.minus(s)]
        self.seeds = pairs[: 2 * groups // TURNS]
        self.list = [self.turn(h, i) for h in range(TURNS) for i in range(len(self.seeds))]
        used = set(self.list)
        spots.sort(key=lambda s: (-self.hops(s), min(s, self.minus(s))))
        rest = [(*s, c) for s in spots for c in range(2) if (*s, c) not in used]
        self.list += [p for p in rest if any(p)] + [(0, 0, 0, 0)]
        self.index = {p: t for t, p in enumerate(self.list)}

    def hops(self, spot):
        return sum(min(v, n - v) for v, n in zip(spot, self.sizes))

    def minus(self, spot):
        return tuple(-v % n for v, n in zip(spot, self.sizes))

    def turn(self, h, i):
        spot = self.seeds[i]
        return (*(self.minus(spot) if (h // 2 + i) % 2 else spot), h % 2)

    def back(self, t):
        *spot, c = self.list[t]
        return self.index[(*self.minus(spot), c)]

    def codes(self):
        return np.array([[((x * self.side + z) * self.side + y) * 2 + c] for x, y, z, c in self.list], np.int32)


class Here:
    def __init__(self, places):
        self.places = places
        side = places.side
        brick = lax.axis_index("brick")
        self.x, self.c = lax.axis_index("dom"), brick % 2
        self.y, self.z = (brick // 2) % side, brick // (2 * side)
        self.xs = [(self.x + k) % places.doms for k in range(places.doms)]
        self.ys = [((self.y + k) % side) * 2 for k in range(side)]
        self.zs = [((self.z + k) % side) * (2 * side) for k in range(side)]
        self.cs = [(self.c + k) % 2 for k in range(2)]

    def coords(self, x, y, z, c):
        side = self.places.side
        brick = ((self.z + z) % side) * (2 * side) + ((self.y + y) % side) * 2 + (self.c + c) % 2
        return (self.x + x) % self.places.doms, brick

    def at(self, t):
        x, y, z, c = self.places.list[t]
        return self.xs[x], self.zs[z] + self.ys[y] + self.cs[c]

    def in_turn(self, h, i):
        sign = 1 + 2 * ((h // 2 + i) % 2)
        x, y, z = self.places.seeds[i]
        return self.coords(sign * x, sign * y, sign * z, h % 2)


def rows(values):
    it = lax.broadcasted_iota(jnp.int32, (8, 128), 0)
    out = jnp.zeros((8, 128), F32)
    for k, v in enumerate(values):
        if v != 0.0:
            out = jnp.where(it == k, F32(v), out)
    return out


def split3(z):
    h = z.astype(BF16).astype(F32)
    r = z - h
    m = r.astype(BF16).astype(F32)
    return h, m, r - m


def split2(z):
    h = z.astype(BF16)
    return h, (z - h.astype(F32)).astype(BF16)


def upper(n, strict_lower=False):
    a = lax.broadcasted_iota(jnp.int32, (n, n), 0)
    b = lax.broadcasted_iota(jnp.int32, (n, n), 1)
    return ((a > b) if strict_lower else (a < b)).astype(F32).astype(BF16)


def dot(a, b):
    return jnp.dot(a, b, preferred_element_type=F32)


def main_kernel(
    codes, peers, remotes, locals_, pos, dirn, mask,
    came, sums_out, asked_out,
    own, f8, lhs, request, asked, order, table, order_s, table_s, send, early, late, right, left, give,
    cs0, cs1, ws0, ws1, sems, *, places,
):
    here = Here(places)
    count = places.count
    cap = send.shape[0] // count
    npairs, nb = mask.shape[0], pos.shape[1]
    groups = npairs // GROUP
    per_turn = groups // TURNS
    self_t = count - 1
    split = early.shape[0] // cap
    barrier = pltpu.get_barrier_semaphore()
    for t in range(self_t):
        pl.semaphore_signal(barrier, inc=1, device_id=here.at(t), device_id_type=MESH)

    x = [pos[c] - 0.5 for c in range(3)]
    u = [dirn[c] for c in range(3)]
    a = x[0] * x[0] + x[1] * x[1] + x[2] * x[2] + 0.1
    b = x[0] * u[0] + x[1] * u[1] + x[2] * u[2]
    for k, v in enumerate(x + u + [jnp.ones_like(a), jnp.zeros_like(a)]):
        own[:, k, :] = v
    for k, v in enumerate(x + [a, b] + u):
        f8[:, k, :] = v

    peer = peers[...]
    remote = remotes[...].astype(F32)
    local = locals_[...].astype(F32)
    side = places.side
    cx = codes[...] // (2 * side * side)
    cz = (codes[...] // (2 * side)) % side
    cy = (codes[...] // 2) % side
    cc = codes[...] % 2
    device = (
        ((here.x + cx) % places.doms) * places.bricks
        + ((here.z + cz) % side) * (2 * side) + ((here.y + cy) % side) * 2 + (here.c + cc) % 2
    )
    hot = jnp.where(device == peer, 1.0, 0.0)
    hot16 = hot.astype(BF16)
    before = dot(hot16, upper(npairs))
    base = jnp.sum(dot(upper(count, True), hot16), axis=1, keepdims=True)
    place = lax.broadcasted_iota(jnp.int32, (count, npairs), 0).astype(F32)
    rank = jnp.sum(hot * before, axis=0, keepdims=True)
    where_t = jnp.sum(hot * place, axis=0, keepdims=True)
    sorted_k = jnp.sum(hot * (before + base), axis=0, keepdims=True)
    it256 = lax.broadcasted_iota(jnp.int32, (npairs, npairs), 0).astype(F32)
    moved = jnp.where(it256 == sorted_k, 1.0, 0.0).astype(BF16)
    number = lax.broadcasted_iota(jnp.int32, (1, npairs), 1).astype(F32)
    sub = lax.broadcasted_iota(jnp.int32, (8, npairs), 0)
    values = jnp.zeros((8, npairs), F32)
    for k, v in enumerate([where_t, rank, local, number]):
        values = jnp.where(sub == k, v, values)
    values = lax.dot_general(values.astype(BF16), moved, NT, preferred_element_type=F32)
    values = jnp.where(sub == 1, values[1:2] + cap * values[0:1], values)
    order[...] = values.astype(jnp.int32)
    wanted = hot * (remote + 1.0)
    lane = lax.broadcasted_iota(jnp.int32, (count, 128), 1)
    out = jnp.where(lane == cap, base, 0.0)
    for r in range(cap):
        named = jnp.sum(jnp.where(before == r, wanted, 0.0), axis=1, keepdims=True)
        out = jnp.where(lane == r, named, out)
    request[...] = out
    to_order = pltpu.make_async_copy(order, order_s, sems.at[2])
    to_order.start()

    pl.semaphore_wait(barrier, count - 1)
    for t in range(self_t):
        pltpu.make_async_remote_copy(
            src_ref=request.at[pl.ds(t, 1)], dst_ref=asked.at[pl.ds(places.back(t), 1)],
            send_sem=sems.at[0], recv_sem=sems.at[1], device_id=here.at(t), device_id_type=MESH,
        ).start()

    eye = (
        lax.broadcasted_iota(jnp.int32, (128, 128), 0) == lax.broadcasted_iota(jnp.int32, (128, 128), 1)
    ).astype(F32).astype(BF16)
    ones3 = rows([1, 1, 1])
    zero = jnp.zeros((8, 128), F32)

    @pl.loop(0, nb // 8)
    def _(g):
        for j in range(8):
            k = g * 8 + j
            h, m, l = split3(f8[k])
            fk = jnp.concatenate([h, h, m, m, h, l, ones3, ones3, ones3, zero], axis=0).astype(BF16)
            lhs[k] = lax.dot_general(eye, fk, NT, preferred_element_type=F32).astype(BF16)

    right[pl.ds(npairs, 8)] = jnp.zeros((8, 8, 128), F32)
    to_order.wait()
    rest = pltpu.make_async_remote_copy(
        src_ref=request.at[pl.ds(0, self_t)], dst_ref=asked.at[pl.ds(0, self_t)],
        send_sem=sems.at[0], recv_sem=sems.at[1], device_id=here.at(0), device_id_type=MESH,
    )
    rest.wait_recv()
    at_place = lax.broadcasted_iota(jnp.int32, (count, 128), 0)
    both = jnp.where(at_place == self_t, request[...], jnp.where(at_place < self_t, asked[...], 0.0)).T
    bases = request[...].T
    sub8 = lax.broadcasted_iota(jnp.int32, (8, count), 0)
    table[...] = jnp.where(sub8 < cap, both[:8], bases[:8]).astype(jnp.int32)
    asked_out[...] = table[...]
    to_scalars = pltpu.make_async_copy(table, table_s, sems.at[2])
    to_scalars.start()
    to_scalars.wait()

    def slots(t):
        return pl.ds(cap * t, cap)

    for t in range(count):
        for r in range(cap):
            send[cap * t + r] = own[jnp.clip(table_s[r, t] - 1, 0, nb - 1)]
        if t < self_t:
            back = places.back(t)
            dst, sem = (early.at[slots(back)], 4) if back < split else (late.at[slots(back - split)], 7)
            pltpu.make_async_remote_copy(
                src_ref=send.at[slots(t), pl.ds(0, 6)], dst_ref=dst.at[:, pl.ds(0, 6)],
                send_sem=sems.at[3], recv_sem=sems.at[sem], device_id=here.at(t), device_id_type=MESH,
            ).start()
    kept = pltpu.make_async_copy(
        send.at[slots(self_t), pl.ds(0, 6)], late.at[slots(self_t - split), pl.ds(0, 6)], sems.at[2]
    )
    kept.start()
    kept.wait()
    rest.wait_send()
    sent = pltpu.make_async_remote_copy(
        src_ref=send.at[pl.ds(0, cap * self_t), pl.ds(0, 6)], dst_ref=give.at[pl.ds(0, cap * self_t), pl.ds(0, 6)],
        send_sem=sems.at[3], recv_sem=sems.at[4], device_id=here.at(0), device_id_type=MESH,
    )

    def arrival(ref, places_in, sem):
        part = ref.at[pl.ds(0, cap * places_in), pl.ds(0, 6)]
        return pltpu.make_async_remote_copy(
            src_ref=part, dst_ref=part, send_sem=sems.at[3], recv_sem=sems.at[sem],
            device_id=here.at(0), device_id_type=MESH,
        )

    arrival(early, split, 4).wait_recv()

    it = lax.broadcasted_iota(jnp.int32, (8, 128), 0)
    lane128 = lax.broadcasted_iota(jnp.int32, (128, 128), 1)
    top = rows([0, 0, 0, 0, 0, 0, 1])
    cp = rows([-2, -2, -2])
    e3 = rows([0, 0, 0, 1])
    e34 = rows([0, 0, 0, 1, 1])
    last = rows([0, 0, 0, 0, 0, 0, 0, 1])
    m35 = rows([0, 0, 0, 1, 1, 1])
    cs, ws = (cs0, cs1), (ws0, ws1)

    def whole(row):
        return jnp.broadcast_to(row, (8, 128))

    def spread(z):
        h, m, l = split3(z)
        return [h, m, h, m, l, h]

    def halves(z):
        h, l, _ = split3(z)
        return jnp.concatenate([h, l], axis=0).astype(BF16)

    def block(p):
        return jnp.clip(order_s[2, p], 0, nb - 1)

    def other(p, first):
        q = order_s[1, p]
        found = early[jnp.clip(q, 0, cap * split - 1)]
        if not first:
            found = jnp.where(q < cap * split, found, late[jnp.clip(q - cap * split, 0, cap * (count - split) - 1)])
        return jnp.where(it < 6, found, top)

    def active(p):
        return whole(mask[pl.ds(jnp.clip(order_s[3, p], 0, npairs - 1), 1), :].astype(F32))

    def distances(p, first):
        b = other(p, first)
        ro = pltpu.roll(b, 5, 0)
        rp = jnp.concatenate(spread(b * cp + e3) + list(split3(b * b)) + [zero], axis=0).astype(BF16)
        rq = jnp.concatenate(spread(e34 - ro) + list(split3(b * ro)) + [zero], axis=0).astype(BF16)
        return dot(lhs[block(p)], jnp.concatenate([rp, rq], axis=1))

    def factors(p, j, given, c, w, first):
        b = other(p, first)
        for i in range(0, 128, 16):
            s = jnp.minimum(given[i : i + 16, 0:128], 1.0)
            l2 = F32(2.0 * math.log(2.0)) * jnp.log2(s)
            t = 1.0 - 1.0 / s
            c1h, c1l = split2((s - 1.0) * (l2 + t))
            c2h, c2l = split2((t * (t - 4.0) - l2) * given[i : i + 16, 128:256])
            hi, lo = pl.ds(256 * j + i, 16), pl.ds(256 * j + 128 + i, 16)
            c[hi, 0:128] = c1h
            c[hi, 128:256] = c2h
            c[lo, 0:128] = c1l
            c[lo, 128:256] = c2l
        x = halves(own[block(p)] * active(p))
        r = dot(jnp.concatenate([x, x], axis=1), c[pl.ds(256 * j, 256), :])
        r = r[:8] + r[8:]
        r1, r2 = r[:, :128], r[:, 128:]
        d1 = r1 - b * whole(r1[6:7])
        d2 = r2 - b * whole(r2[6:7])
        right[p] = (-K1) * d1 - K2 * m35 * pltpu.roll(d2, 3, 0)
        w[pl.ds(16 * j, 16), 0:128] = halves(K1 * b)
        w[pl.ds(16 * j, 16), 128:256] = halves(K2 * (m35 * pltpu.roll(b, 3, 0) + last))

    def residents(g, c, w):
        res = lax.dot_general(c[...], w[...], NT, preferred_element_type=F32)
        tot = res[:128] + res[128:256]
        for j in range(1, GROUP):
            tot = jnp.where(
                lane128 >= 16 * j, res[256 * j : 256 * j + 128] + res[256 * j + 128 : 256 * j + 256], tot
            )
        tr = tot.T
        for j in range(GROUP):
            p = g * GROUP + j
            o = own[block(p)]
            sums = tr[16 * j : 16 * j + 8] + tr[16 * j + 8 : 16 * j + 16]
            term = o * whole(sums[6:7]) + m35 * pltpu.roll(o, 3, 0) * whole(sums[7:8]) - sums
            left[p] = active(p) * term

    def hand_back(t, back, to):
        first = jnp.clip(table_s[cap, t], 0, npairs)
        for r in range(cap):
            give[cap * t + r] = right[first + r]
        return pltpu.make_async_remote_copy(
            src_ref=give.at[slots(t), pl.ds(0, 6)], dst_ref=came.at[slots(back), pl.ds(0, 6)],
            send_sem=sems.at[5], recv_sem=sems.at[6], device_id=to, device_id_type=MESH,
        ).start()

    def turn(h, first):
        start = per_turn * GROUP * h
        ahead = [distances(start + n, first) for n in range(AHEAD)]
        for k in range(per_turn):
            odd = k % 2
            g = per_turn * h + k
            if not first or k > 0:
                residents(g - 1, cs[1 - odd], ws[1 - odd])
            for j in range(GROUP):
                n = k * GROUP + j
                if n + AHEAD < per_turn * GROUP:
                    ahead.append(distances(start + n + AHEAD, first))
                factors(start + n, j, ahead.pop(0), cs[odd], ws[odd], first)
        for i in range(2 * per_turn):
            hand_back(h * 2 * per_turn + i, ((h + 2) % TURNS) * 2 * per_turn + i, here.in_turn(h, i))

    turn(0, True)
    arrival(late, self_t - split, 7).wait_recv()

    @pl.loop(1, TURNS)
    def _(h):
        turn(h, False)

    for t in range(2 * groups, self_t):
        hand_back(t, places.back(t), here.at(t))
    first = jnp.clip(table_s[cap, self_t], 0, npairs)
    for r in range(cap):
        give[cap * self_t + r] = right[first + r]
    kept = pltpu.make_async_copy(
        give.at[slots(self_t), pl.ds(0, 6)], came.at[slots(self_t), pl.ds(0, 6)], sems.at[2]
    )
    kept.start()
    residents(groups - 1, cs1, ws1)
    block_of = lax.broadcasted_iota(jnp.int32, (nb, npairs), 0)
    chosen = jnp.where(block_of == order[2:3, :], 1.0, 0.0).astype(BF16)
    for c in range(6):
        parts = jnp.concatenate(split3(left[:, c, :]), axis=1).astype(BF16)
        sums = dot(chosen, parts)
        sums_out[c] = sums[:, :128] + sums[:, 128:256] + sums[:, 256:]
    kept.wait()
    sent.wait_send()
    final = pltpu.make_async_remote_copy(
        src_ref=give.at[pl.ds(0, cap * self_t), pl.ds(0, 6)], dst_ref=came.at[pl.ds(0, cap * self_t), pl.ds(0, 6)],
        send_sem=sems.at[5], recv_sem=sems.at[6], device_id=here.at(0), device_id_type=MESH,
    )
    final.wait_recv()
    final.wait_send()


def add_kernel(asked, sums, came, grad, hess, *parts, cap):
    step = pl.program_id(0)
    blocks = parts[0].shape[0] - 1
    here = came.shape[0] // cap

    @pl.when(step == 0)
    def _():
        for part in parts:
            part[...] = jnp.zeros_like(part)

    @pl.loop(0, here // 8)
    def _(g):
        for j in range(8):
            d = g * 8 + j
            for r in range(cap):
                a = asked[r, step * here + d]
                k = jnp.where(a > 0, a - 1, blocks)
                parts[(j * cap + r) % len(parts)][k] += came[cap * d + r]

    @pl.when(step == pl.num_programs(0) - 1)
    def _():
        total = parts[0][:blocks]
        for part in parts[1:]:
            total = total + part[:blocks]
        parts[0][:blocks] = total
        for c in range(3):
            grad[c] = parts[0][:blocks, c] + sums[c]
            hess[c] = parts[0][:blocks, 3 + c] + sums[3 + c]


def on_device(positions, direction, pair_local, pair_peer, pair_remote, pair_mask, *, shape):
    npairs = pair_local.shape[0]
    nb, width = positions.shape[1:]
    places = Places(*shape, npairs // GROUP)
    count = places.count
    cap = max(2, 2 * npairs // count)
    V = pl.BlockSpec(memory_space=pltpu.VMEM)
    S = pl.BlockSpec(memory_space=pltpu.SMEM)
    A = pl.BlockSpec(memory_space=pl.ANY)
    params = functools.partial(pltpu.CompilerParams, vmem_limit_bytes=60 * 2**20)
    tiles = lambda n: pltpu.VMEM((n, 8, width), F32)
    row = lambda v: v.reshape(1, npairs)
    reach = npairs // TURNS - 1 + count * cap - npairs
    split = reach // cap + 1
    came, sums, asked = pl.pallas_call(
        functools.partial(main_kernel, places=places),
        out_shape=(
            jax.ShapeDtypeStruct((count * cap, 8, width), F32),
            jax.ShapeDtypeStruct((6, nb, width), F32),
            jax.ShapeDtypeStruct((8, count), jnp.int32),
        ),
        in_specs=[V] * 7,
        out_specs=(A, V, V),
        scratch_shapes=[
            tiles(nb), tiles(nb), pltpu.VMEM((nb, width, DEPTH), BF16),
            pltpu.VMEM((count, 128), F32), pltpu.VMEM((count, 128), F32),
            pltpu.VMEM((8, npairs), jnp.int32), pltpu.VMEM((8, count), jnp.int32),
            pltpu.SMEM((8, npairs), jnp.int32), pltpu.SMEM((8, count), jnp.int32),
            tiles(count * cap), tiles(cap * split), tiles(cap * (count - split)),
            tiles(npairs + 8), tiles(npairs), tiles(count * cap),
            *[pltpu.VMEM((256 * GROUP, 256), BF16)] * 2,
            *[pltpu.VMEM((16 * GROUP, 256), BF16)] * 2,
            pltpu.SemaphoreType.DMA((8,)),
        ],
        compiler_params=params(collective_id=0, has_side_effects=True),
        name="main",
    )(places.codes(), row(pair_peer), row(pair_remote), row(pair_local), positions, direction, pair_mask)
    half = jax.ShapeDtypeStruct((3, nb, width), F32)
    chunks = 4
    return pl.pallas_call(
        functools.partial(add_kernel, cap=cap),
        out_shape=(half, half),
        grid=(chunks,),
        in_specs=[S, V, pl.BlockSpec((count * cap // chunks, 8, width), lambda i: (i, 0, 0))],
        out_specs=(V, V),
        scratch_shapes=[tiles(nb + 1)] * 8,
        compiler_params=params(),
        name="add",
    )(asked, sums, came)


def solution(mesh):
    shape = (mesh.shape["dom"], mesh.shape["brick"])
    rows_of = P(None, AXES, None)
    return jax.shard_map(
        functools.partial(on_device, shape=shape),
        mesh=mesh,
        in_specs=(rows_of, rows_of, P(AXES), P(AXES, None), P(AXES), P(AXES, None)),
        out_specs=(rows_of, rows_of),
        check_vma=False,
    )
```

```python
import functools
import itertools
import math

import jax
import jax.numpy as jnp
import numpy as np
from jax import lax
from jax.experimental import pallas as pl
from jax.experimental.pallas import tpu as pltpu
from jax.sharding import PartitionSpec as P

F32, BF16 = jnp.float32, jnp.bfloat16
MESH = pl.DeviceIdType.MESH
AXES = ("dom", "brick")
NT = (((1,), (1,)), ((), ()))
K1, K2 = -0.01, 0.02
DEPTH = 80
GROUP = 8
TURNS = 4
AHEAD = 4


class Places:
    def __init__(self, doms, bricks, groups):
        side = math.isqrt(bricks // 2)
        self.doms, self.bricks, self.side = doms, bricks, side
        self.count = doms * bricks
        self.sizes = (doms, side, side)
        spots = sorted(itertools.product(*map(range, self.sizes)), key=lambda s: (-self.hops(s), -len(set(s)), s))
        pairs = [s for s in spots if self.minus(s) != s and s < self.minus(s)]
        self.seeds = pairs[: 2 * groups // TURNS]
        self.list = [self.turn(h, i) for h in range(TURNS) for i in range(len(self.seeds))]
        used = set(self.list)
        spots.sort(key=lambda s: (-self.hops(s), min(s, self.minus(s))))
        rest = [(*s, c) for s in spots for c in range(2) if (*s, c) not in used]
        self.list += [p for p in rest if any(p)] + [(0, 0, 0, 0)]
        self.index = {p: t for t, p in enumerate(self.list)}

    def hops(self, spot):
        return sum(min(v, n - v) for v, n in zip(spot, self.sizes))

    def minus(self, spot):
        return tuple(-v % n for v, n in zip(spot, self.sizes))

    def turn(self, h, i):
        spot = self.seeds[i]
        return (*(self.minus(spot) if (h // 2 + i) % 2 else spot), h % 2)

    def back(self, t):
        *spot, c = self.list[t]
        return self.index[(*self.minus(spot), c)]

    def codes(self):
        return np.array([[((x * self.side + z) * self.side + y) * 2 + c] for x, y, z, c in self.list], np.int32)


class Here:
    def __init__(self, places):
        self.places = places
        side = places.side
        brick = lax.axis_index("brick")
        self.x, self.c = lax.axis_index("dom"), brick % 2
        self.y, self.z = (brick // 2) % side, brick // (2 * side)
        self.xs = [(self.x + k) % places.doms for k in range(places.doms)]
        self.ys = [((self.y + k) % side) * 2 for k in range(side)]
        self.zs = [((self.z + k) % side) * (2 * side) for k in range(side)]
        self.cs = [(self.c + k) % 2 for k in range(2)]

    def coords(self, x, y, z, c):
        side = self.places.side
        brick = ((self.z + z) % side) * (2 * side) + ((self.y + y) % side) * 2 + (self.c + c) % 2
        return (self.x + x) % self.places.doms, brick

    def at(self, t):
        x, y, z, c = self.places.list[t]
        return self.xs[x], self.zs[z] + self.ys[y] + self.cs[c]

    def in_turn(self, h, i):
        sign = 1 + 2 * ((h // 2 + i) % 2)
        x, y, z = self.places.seeds[i]
        return self.coords(sign * x, sign * y, sign * z, h % 2)


def rows(values):
    it = lax.broadcasted_iota(jnp.int32, (8, 128), 0)
    out = jnp.zeros((8, 128), F32)
    for k, v in enumerate(values):
        if v != 0.0:
            out = jnp.where(it == k, F32(v), out)
    return out


def split3(z):
    h = z.astype(BF16).astype(F32)
    r = z - h
    m = r.astype(BF16).astype(F32)
    return h, m, r - m


def split2(z):
    h = z.astype(BF16)
    return h, (z - h.astype(F32)).astype(BF16)


def upper(n, strict_lower=False):
    a = lax.broadcasted_iota(jnp.int32, (n, n), 0)
    b = lax.broadcasted_iota(jnp.int32, (n, n), 1)
    return ((a > b) if strict_lower else (a < b)).astype(F32).astype(BF16)


def dot(a, b):
    return jnp.dot(a, b, preferred_element_type=F32)


def main_kernel(
    codes, peers, remotes, locals_, pos, dirn, mask,
    came, sums_out, asked_out,
    own, f8, lhs, request, asked, order, table, order_s, table_s, send, early, late, right, left, give,
    cs0, cs1, ws0, ws1, sems, *, places,
):
    here = Here(places)
    count = places.count
    cap = send.shape[0] // count
    npairs, nb = mask.shape[0], pos.shape[1]
    groups = npairs // GROUP
    per_turn = groups // TURNS
    self_t = count - 1
    split = early.shape[0] // cap
    barrier = pltpu.get_barrier_semaphore()
    for t in range(self_t):
        pl.semaphore_signal(barrier, inc=1, device_id=here.at(t), device_id_type=MESH)

    peer = peers[...]
    remote = remotes[...].astype(F32)
    local = locals_[...].astype(F32)
    side = places.side
    cx = codes[...] // (2 * side * side)
    cz = (codes[...] // (2 * side)) % side
    cy = (codes[...] // 2) % side
    cc = codes[...] % 2
    device = (
        ((here.x + cx) % places.doms) * places.bricks
        + ((here.z + cz) % side) * (2 * side) + ((here.y + cy) % side) * 2 + (here.c + cc) % 2
    )
    hot = jnp.where(device == peer, 1.0, 0.0)
    hot16 = hot.astype(BF16)
    before = dot(hot16, upper(npairs))
    base = jnp.sum(dot(upper(count, True), hot16), axis=1, keepdims=True)
    wanted = hot * (remote + 1.0)
    lane = lax.broadcasted_iota(jnp.int32, (count, 128), 1)
    out = jnp.where(lane == cap, base, 0.0)
    for r in range(cap):
        named = jnp.sum(jnp.where(before == r, wanted, 0.0), axis=1, keepdims=True)
        out = jnp.where(lane == r, named, out)
    request[...] = out

    pl.semaphore_wait(barrier, count - 1)
    for t in range(self_t):
        pltpu.make_async_remote_copy(
            src_ref=request.at[pl.ds(t, 1)], dst_ref=asked.at[pl.ds(places.back(t), 1)],
            send_sem=sems.at[0], recv_sem=sems.at[1], device_id=here.at(t), device_id_type=MESH,
        ).start()

    x = [pos[c] - 0.5 for c in range(3)]
    u = [dirn[c] for c in range(3)]
    a = x[0] * x[0] + x[1] * x[1] + x[2] * x[2] + 0.1
    b = x[0] * u[0] + x[1] * u[1] + x[2] * u[2]
    for k, v in enumerate(x + u + [jnp.ones_like(a), jnp.zeros_like(a)]):
        own[:, k, :] = v
    for k, v in enumerate(x + [a, b] + u):
        f8[:, k, :] = v

    rest = pltpu.make_async_remote_copy(
        src_ref=request.at[pl.ds(0, self_t)], dst_ref=asked.at[pl.ds(0, self_t)],
        send_sem=sems.at[0], recv_sem=sems.at[1], device_id=here.at(0), device_id_type=MESH,
    )
    rest.wait_recv()
    at_place = lax.broadcasted_iota(jnp.int32, (count, 128), 0)
    both = jnp.where(at_place == self_t, request[...], jnp.where(at_place < self_t, asked[...], 0.0)).T
    bases = request[...].T
    sub8 = lax.broadcasted_iota(jnp.int32, (8, count), 0)
    table[...] = jnp.where(sub8 < cap, both[:8], bases[:8]).astype(jnp.int32)
    asked_out[...] = table[...]
    to_scalars = pltpu.make_async_copy(table, table_s, sems.at[2])
    to_scalars.start()
    to_scalars.wait()

    def slots(t):
        return pl.ds(cap * t, cap)

    for t in range(count):
        for r in range(cap):
            send[cap * t + r] = own[jnp.clip(table_s[r, t] - 1, 0, nb - 1)]
        if t < self_t:
            back = places.back(t)
            dst, sem = (early.at[slots(back)], 4) if back < split else (late.at[slots(back - split)], 7)
            pltpu.make_async_remote_copy(
                src_ref=send.at[slots(t), pl.ds(0, 6)], dst_ref=dst.at[:, pl.ds(0, 6)],
                send_sem=sems.at[3], recv_sem=sems.at[sem], device_id=here.at(t), device_id_type=MESH,
            ).start()
    kept = pltpu.make_async_copy(
        send.at[slots(self_t), pl.ds(0, 6)], late.at[slots(self_t - split), pl.ds(0, 6)], sems.at[2]
    )
    kept.start()
    kept.wait()
    rest.wait_send()
    place = lax.broadcasted_iota(jnp.int32, (count, npairs), 0).astype(F32)
    rank = jnp.sum(hot * before, axis=0, keepdims=True)
    where_t = jnp.sum(hot * place, axis=0, keepdims=True)
    sorted_k = jnp.sum(hot * (before + base), axis=0, keepdims=True)
    it256 = lax.broadcasted_iota(jnp.int32, (npairs, npairs), 0).astype(F32)
    moved = jnp.where(it256 == sorted_k, 1.0, 0.0).astype(BF16)
    number = lax.broadcasted_iota(jnp.int32, (1, npairs), 1).astype(F32)
    sub = lax.broadcasted_iota(jnp.int32, (8, npairs), 0)
    values = jnp.zeros((8, npairs), F32)
    for k, v in enumerate([where_t, rank, local, number]):
        values = jnp.where(sub == k, v, values)
    values = lax.dot_general(values.astype(BF16), moved, NT, preferred_element_type=F32)
    values = jnp.where(sub == 1, values[1:2] + cap * values[0:1], values)
    order[...] = values.astype(jnp.int32)
    to_order = pltpu.make_async_copy(order, order_s, sems.at[2])
    to_order.start()
    eye = (
        lax.broadcasted_iota(jnp.int32, (128, 128), 0) == lax.broadcasted_iota(jnp.int32, (128, 128), 1)
    ).astype(F32).astype(BF16)
    ones3 = rows([1, 1, 1])
    zero = jnp.zeros((8, 128), F32)

    @pl.loop(0, nb // 8)
    def _(g):
        for j in range(8):
            k = g * 8 + j
            h, m, l = split3(f8[k])
            fk = jnp.concatenate([h, h, m, m, h, l, ones3, ones3, ones3, zero], axis=0).astype(BF16)
            lhs[k] = lax.dot_general(eye, fk, NT, preferred_element_type=F32).astype(BF16)

    right[pl.ds(npairs, 8)] = jnp.zeros((8, 8, 128), F32)
    to_order.wait()
    sent = pltpu.make_async_remote_copy(
        src_ref=send.at[pl.ds(0, cap * self_t), pl.ds(0, 6)], dst_ref=give.at[pl.ds(0, cap * self_t), pl.ds(0, 6)],
        send_sem=sems.at[3], recv_sem=sems.at[4], device_id=here.at(0), device_id_type=MESH,
    )

    def arrival(ref, places_in, sem):
        part = ref.at[pl.ds(0, cap * places_in), pl.ds(0, 6)]
        return pltpu.make_async_remote_copy(
            src_ref=part, dst_ref=part, send_sem=sems.at[3], recv_sem=sems.at[sem],
            device_id=here.at(0), device_id_type=MESH,
        )

    arrival(early, split, 4).wait_recv()

    it = lax.broadcasted_iota(jnp.int32, (8, 128), 0)
    lane128 = lax.broadcasted_iota(jnp.int32, (128, 128), 1)
    top = rows([0, 0, 0, 0, 0, 0, 1])
    cp = rows([-2, -2, -2])
    e3 = rows([0, 0, 0, 1])
    e34 = rows([0, 0, 0, 1, 1])
    last = rows([0, 0, 0, 0, 0, 0, 0, 1])
    m35 = rows([0, 0, 0, 1, 1, 1])
    cs, ws = (cs0, cs1), (ws0, ws1)

    def whole(row):
        return jnp.broadcast_to(row, (8, 128))

    def spread(z):
        h, m, l = split3(z)
        return [h, m, h, m, l, h]

    def halves(z):
        h, l, _ = split3(z)
        return jnp.concatenate([h, l], axis=0).astype(BF16)

    def block(p):
        return jnp.clip(order_s[2, p], 0, nb - 1)

    def other(p, first):
        q = order_s[1, p]
        found = early[jnp.clip(q, 0, cap * split - 1)]
        if not first:
            found = jnp.where(q < cap * split, found, late[jnp.clip(q - cap * split, 0, cap * (count - split) - 1)])
        return jnp.where(it < 6, found, top)

    def active(p):
        return whole(mask[pl.ds(jnp.clip(order_s[3, p], 0, npairs - 1), 1), :].astype(F32))

    def distances(p, first):
        b = other(p, first)
        ro = pltpu.roll(b, 5, 0)
        rp = jnp.concatenate(spread(b * cp + e3) + list(split3(b * b)) + [zero], axis=0).astype(BF16)
        rq = jnp.concatenate(spread(e34 - ro) + list(split3(b * ro)) + [zero], axis=0).astype(BF16)
        return dot(lhs[block(p)], jnp.concatenate([rp, rq], axis=1))

    def factors(p, j, given, c, w, first):
        b = other(p, first)
        for i in range(0, 128, 16):
            s = jnp.minimum(given[i : i + 16, 0:128], 1.0)
            l2 = F32(2.0 * math.log(2.0)) * jnp.log2(s)
            t = 1.0 - 1.0 / s
            c1h, c1l = split2((s - 1.0) * (l2 + t))
            c2h, c2l = split2((t * (t - 4.0) - l2) * given[i : i + 16, 128:256])
            hi, lo = pl.ds(256 * j + i, 16), pl.ds(256 * j + 128 + i, 16)
            c[hi, 0:128] = c1h
            c[hi, 128:256] = c2h
            c[lo, 0:128] = c1l
            c[lo, 128:256] = c2l
        x = halves(own[block(p)] * active(p))
        r = dot(jnp.concatenate([x, x], axis=1), c[pl.ds(256 * j, 256), :])
        r = r[:8] + r[8:]
        r1, r2 = r[:, :128], r[:, 128:]
        d1 = r1 - b * whole(r1[6:7])
        d2 = r2 - b * whole(r2[6:7])
        right[p] = (-K1) * d1 - K2 * m35 * pltpu.roll(d2, 3, 0)
        w[pl.ds(16 * j, 16), 0:128] = halves(K1 * b)
        w[pl.ds(16 * j, 16), 128:256] = halves(K2 * (m35 * pltpu.roll(b, 3, 0) + last))

    def residents(g, c, w):
        res = lax.dot_general(c[...], w[...], NT, preferred_element_type=F32)
        tot = res[:128] + res[128:256]
        for j in range(1, GROUP):
            tot = jnp.where(
                lane128 >= 16 * j, res[256 * j : 256 * j + 128] + res[256 * j + 128 : 256 * j + 256], tot
            )
        tr = tot.T
        for j in range(GROUP):
            p = g * GROUP + j
            o = own[block(p)]
            sums = tr[16 * j : 16 * j + 8] + tr[16 * j + 8 : 16 * j + 16]
            term = o * whole(sums[6:7]) + m35 * pltpu.roll(o, 3, 0) * whole(sums[7:8]) - sums
            left[p] = active(p) * term

    def hand_back(t, back, to):
        first = jnp.clip(table_s[cap, t], 0, npairs)
        for r in range(cap):
            give[cap * t + r] = right[first + r]
        return pltpu.make_async_remote_copy(
            src_ref=give.at[slots(t), pl.ds(0, 6)], dst_ref=came.at[slots(back), pl.ds(0, 6)],
            send_sem=sems.at[5], recv_sem=sems.at[6], device_id=to, device_id_type=MESH,
        ).start()

    def turn(h, first):
        start = per_turn * GROUP * h
        ahead = [distances(start + n, first) for n in range(AHEAD)]
        for k in range(per_turn):
            odd = k % 2
            g = per_turn * h + k
            if not first or k > 0:
                residents(g - 1, cs[1 - odd], ws[1 - odd])
            for j in range(GROUP):
                n = k * GROUP + j
                if n + AHEAD < per_turn * GROUP:
                    ahead.append(distances(start + n + AHEAD, first))
                factors(start + n, j, ahead.pop(0), cs[odd], ws[odd], first)
        for i in range(2 * per_turn):
            hand_back(h * 2 * per_turn + i, ((h + 2) % TURNS) * 2 * per_turn + i, here.in_turn(h, i))

    turn(0, True)
    arrival(late, self_t - split, 7).wait_recv()

    @pl.loop(1, TURNS)
    def _(h):
        turn(h, False)

    for t in range(2 * groups, self_t):
        hand_back(t, places.back(t), here.at(t))
    first = jnp.clip(table_s[cap, self_t], 0, npairs)
    for r in range(cap):
        give[cap * self_t + r] = right[first + r]
    kept = pltpu.make_async_copy(
        give.at[slots(self_t), pl.ds(0, 6)], came.at[slots(self_t), pl.ds(0, 6)], sems.at[2]
    )
    kept.start()
    residents(groups - 1, cs1, ws1)
    block_of = lax.broadcasted_iota(jnp.int32, (nb, npairs), 0)
    chosen = jnp.where(block_of == order[2:3, :], 1.0, 0.0).astype(BF16)
    for c in range(6):
        parts = jnp.concatenate(split3(left[:, c, :]), axis=1).astype(BF16)
        sums = dot(chosen, parts)
        sums_out[c] = sums[:, :128] + sums[:, 128:256] + sums[:, 256:]
    kept.wait()
    sent.wait_send()
    final = pltpu.make_async_remote_copy(
        src_ref=give.at[pl.ds(0, cap * self_t), pl.ds(0, 6)], dst_ref=came.at[pl.ds(0, cap * self_t), pl.ds(0, 6)],
        send_sem=sems.at[5], recv_sem=sems.at[6], device_id=here.at(0), device_id_type=MESH,
    )
    final.wait_recv()
    final.wait_send()


def add_kernel(asked, sums, came, grad, hess, *parts, cap):
    step = pl.program_id(0)
    blocks = parts[0].shape[0] - 1
    here = came.shape[0] // cap

    @pl.when(step == 0)
    def _():
        for part in parts:
            part[...] = jnp.zeros_like(part)

    @pl.loop(0, here // 8)
    def _(g):
        for j in range(8):
            d = g * 8 + j
            for r in range(cap):
                a = asked[r, step * here + d]
                k = jnp.where(a > 0, a - 1, blocks)
                parts[(j * cap + r) % len(parts)][k] += came[cap * d + r]

    @pl.when(step == pl.num_programs(0) - 1)
    def _():
        total = parts[0][:blocks]
        for part in parts[1:]:
            total = total + part[:blocks]
        parts[0][:blocks] = total
        for c in range(3):
            grad[c] = parts[0][:blocks, c] + sums[c]
            hess[c] = parts[0][:blocks, 3 + c] + sums[3 + c]


def on_device(positions, direction, pair_local, pair_peer, pair_remote, pair_mask, *, shape):
    npairs = pair_local.shape[0]
    nb, width = positions.shape[1:]
    places = Places(*shape, npairs // GROUP)
    count = places.count
    cap = max(2, 2 * npairs // count)
    V = pl.BlockSpec(memory_space=pltpu.VMEM)
    S = pl.BlockSpec(memory_space=pltpu.SMEM)
    A = pl.BlockSpec(memory_space=pl.ANY)
    params = functools.partial(pltpu.CompilerParams, vmem_limit_bytes=60 * 2**20)
    tiles = lambda n: pltpu.VMEM((n, 8, width), F32)
    row = lambda v: v.reshape(1, npairs)
    reach = npairs // TURNS - 1 + count * cap - npairs
    split = reach // cap + 1
    came, sums, asked = pl.pallas_call(
        functools.partial(main_kernel, places=places),
        out_shape=(
            jax.ShapeDtypeStruct((count * cap, 8, width), F32),
            jax.ShapeDtypeStruct((6, nb, width), F32),
            jax.ShapeDtypeStruct((8, count), jnp.int32),
        ),
        in_specs=[V] * 7,
        out_specs=(A, V, V),
        scratch_shapes=[
            tiles(nb), tiles(nb), pltpu.VMEM((nb, width, DEPTH), BF16),
            pltpu.VMEM((count, 128), F32), pltpu.VMEM((count, 128), F32),
            pltpu.VMEM((8, npairs), jnp.int32), pltpu.VMEM((8, count), jnp.int32),
            pltpu.SMEM((8, npairs), jnp.int32), pltpu.SMEM((8, count), jnp.int32),
            tiles(count * cap), tiles(cap * split), tiles(cap * (count - split)),
            tiles(npairs + 8), tiles(npairs), tiles(count * cap),
            *[pltpu.VMEM((256 * GROUP, 256), BF16)] * 2,
            *[pltpu.VMEM((16 * GROUP, 256), BF16)] * 2,
            pltpu.SemaphoreType.DMA((8,)),
        ],
        compiler_params=params(collective_id=0, has_side_effects=True),
        name="main",
    )(places.codes(), row(pair_peer), row(pair_remote), row(pair_local), positions, direction, pair_mask)
    half = jax.ShapeDtypeStruct((3, nb, width), F32)
    chunks = 2
    return pl.pallas_call(
        functools.partial(add_kernel, cap=cap),
        out_shape=(half, half),
        grid=(chunks,),
        in_specs=[S, V, pl.BlockSpec((count * cap // chunks, 8, width), lambda i: (i, 0, 0))],
        out_specs=(V, V),
        scratch_shapes=[tiles(nb + 1)] * 8,
        compiler_params=params(),
        name="add",
    )(asked, sums, came)


def solution(mesh):
    shape = (mesh.shape["dom"], mesh.shape["brick"])
    rows_of = P(None, AXES, None)
    return jax.shard_map(
        functools.partial(on_device, shape=shape),
        mesh=mesh,
        in_specs=(rows_of, rows_of, P(AXES), P(AXES, None), P(AXES), P(AXES, None)),
        out_specs=(rows_of, rows_of),
        check_vma=False,
    )
```
